1024 devices in a mesh: gx: 4 (over x), gy: 8 (over y, core), ch: 32 (over z).
Axes of the slice: x: 4, y: 4, z: 32, core: 2. Of those that a mesh axis runs over, the one named last changes fastest.
Arguments:
- inputs: bfloat16 [16, 32, 32, 256], P('gx', 'gy', None, 'ch'), may hold values from -6 to 6
- weight: bfloat16 [3, 3, 3, 256, 256], P(None, None, None, 'ch'), may hold values from -0.125 to 0.125
- bias: bfloat16 [256], P('ch'), may hold values from -3 to 3
- cotangent: bfloat16 [16, 32, 32, 256], P('gx', 'gy', None, 'ch'), may hold values from -6 to 6
Outputs:
- activation: bfloat16 [16, 32, 32, 256], P('gx', 'gy', None, 'ch')
- input_grad: bfloat16 [16, 32, 32, 256], P('gx', 'gy', None, 'ch')
- weight_grad: float32 [3, 3, 3, 256, 256], P(None, None, None, 'ch')
- bias_grad: float32 [256], P('ch')
The draws below stay inside these ranges and needn't reach their ends.
All inputs are finite; a program needn't handle non-finite values.
Results may differ from the reference program's by a relative error of at most 0.0075.
Values may be sent and summed in bfloat16 or wider, within the bound.
A program may use at most 32 MiB of HBM per device.

```python
import math
import jax
import jax.numpy as jnp
from jax import lax

CHANNELS = 256
DEPTH = 32
EXTENT_X = 16
EXTENT_Y = 32


def strengthened(array, rng, source, target, parts, factor):
    def block_of(axis_at):
        return (jnp.arange(array.shape[axis_at]) // (array.shape[axis_at] // parts)).reshape((-1,) + (1,) * (array.ndim - 1 - axis_at))

    one_side = jax.random.permutation(rng, parts)[block_of(target)]
    second = (block_of(target) + parts // 2) % parts
    return jnp.where((block_of(source) == one_side) | (block_of(source) == second), factor * array, array)


def block_levels(key, shape, cuts, smallest, high):
    def one(dim, blocks):
        heights = jax.random.uniform(jax.random.fold_in(jax.random.fold_in(key, 6), dim), (blocks,), jnp.float32, smallest / len(cuts), high / len(cuts))
        return jnp.repeat(jnp.exp(heights), shape[dim] // blocks).reshape((-1,) + (1,) * (len(shape) - dim - 1))

    loudness = one(*cuts[0])
    for cut in cuts[1:]:
        loudness = loudness * one(*cut)
    return loudness


def bell_draw(stream_key, extent, scale, bound, split=(), kind=jnp.bfloat16):
    result = scale * jax.random.normal(stream_key, extent, jnp.float32)
    if split:
        result = result * block_levels(stream_key, extent, split, -0.22, 0.18)
    return jnp.clip(result, -bound, bound).astype(kind)


def bell_draw_with(stream_key, extent, spread, reach, shards, heavy, held_as=jnp.bfloat16):
    result = spread * jax.random.normal(stream_key, extent, jnp.float32)
    if shards:
        result = result * block_levels(stream_key, extent, shards, -0.22, 0.18)
    return jnp.clip(strengthened(result, jax.random.fold_in(stream_key, 3), *heavy), -reach, reach).astype(held_as)


def setup_inputs(seed: int = 0) -> dict:
    key_list = jax.random.split(jax.random.key(seed), 5)
    inputs = bell_draw(key_list[0], (EXTENT_X, EXTENT_Y, DEPTH, CHANNELS), 1.0, 6.0, ((0, 4), (1, 8), (3, 32)))
    weight = bell_draw_with(key_list[1], (3, 3, 3, CHANNELS, CHANNELS), (27 * CHANNELS) ** -0.5, 0.125, ((3, 32),), (3, 4, 32, 2.75))
    bias = bell_draw(key_list[2], (CHANNELS,), 0.5, 3.0, ((0, 32),))
    cotangent = bell_draw(key_list[3], (EXTENT_X, EXTENT_Y, DEPTH, CHANNELS), 1.0, 6.0, ((0, 4), (1, 8), (3, 32)))
    return {"inputs": inputs, "weight": weight, "bias": bias, "cotangent": cotangent}


def window(volume, first, second, third, span_x, span_y, span_z):
    piece = volume[first:first + span_x, second:second + span_y, third:third + span_z]
    return piece.reshape(span_x * span_y * span_z, volume.shape[3])

def reference(inputs, weight, bias, cotangent):
    span_x, span_y, span_z, channels = inputs.shape
    volume_cells = span_x * span_y * span_z
    edges = ((1, 1), (1, 1), (1, 1), (0, 0))
    padded = jnp.pad(inputs, edges)
    offsets = [(a, b, c) for a in range(3) for b in range(3) for c in range(3)]
    summed = jnp.zeros((volume_cells, channels), jnp.float32)
    for a, b, c in offsets:
        summed = summed + jnp.dot(window(padded, a, b, c, span_x, span_y, span_z), weight[a, b, c], preferred_element_type=jnp.float32)
    summed = summed + bias.astype(jnp.float32)
    activation = jax.nn.silu(summed).astype(jnp.bfloat16)
    sigmoid_pre = jax.nn.sigmoid(summed)
    slope = (cotangent.reshape(volume_cells, channels).astype(jnp.float32) * sigmoid_pre * (1.0 + summed * (1.0 - sigmoid_pre))).astype(jnp.bfloat16)
    slope_pad = jnp.pad(slope.reshape(span_x, span_y, span_z, channels), edges)
    back_sum = jnp.zeros((volume_cells, channels), jnp.float32)
    grads = []
    for a, b, c in offsets:
        back_sum = back_sum + jnp.dot(window(slope_pad, 2 - a, 2 - b, 2 - c, span_x, span_y, span_z), weight[a, b, c].T, preferred_element_type=jnp.float32)
        grads.append(jnp.dot(window(padded, a, b, c, span_x, span_y, span_z).T, slope, preferred_element_type=jnp.float32))
    factor = 1.0 / math.sqrt(volume_cells)
    weight_grad = jnp.stack(grads).reshape(3, 3, 3, channels, channels) * factor
    bias_grad = lax.optimization_barrier(jnp.sum(slope.astype(jnp.float32), axis=0)) * factor
    return (activation.reshape(inputs.shape), back_sum.astype(jnp.bfloat16).reshape(inputs.shape), weight_grad, bias_grad)
```

```python
import functools
import math

import jax
import jax.numpy as jnp
from jax import lax
from jax.experimental import pallas as pl
from jax.experimental.pallas import tpu as pltpu
from jax.sharding import PartitionSpec as P

MESH = pl.DeviceIdType.MESH
CLASSES = 4
HALO = [(dx, dy) for dx in (-1, 0, 1) for dy in (-1, 0, 1) if (dx, dy) != (0, 0)]
F32 = jnp.float32
BF16 = jnp.bfloat16


def kernel(
    nx, ny, nz, factor,
    x_ref, w_ref, bias_ref, cot_ref,
    act_ref, ig_ref, wg_ref, bg_ref,
    planes, rim, part, near, acc, far, gath, grad, pieces, total, back, back_in,
    halo_s, halo_r, rs1_s, rs1_r, rs2_s, rs2_r, ag1_s, ag1_r, ag2_s, ag2_r,
    wr_s, wr_r, wa_s, wa_r, bk_s, bk_r,
):
    ix, iy, iz = lax.axis_index("gx"), lax.axis_index("gy"), lax.axis_index("ch")
    groups = nz // CLASSES
    half = groups // 2
    peers = nx * ny
    chans = 8 * nz
    cls, grp = lax.rem(iz, CLASSES), lax.div(iz, CLASSES)

    def at_xy(dx, dy):
        return (lax.rem(ix + dx + nx, nx), lax.rem(iy + dy + ny, ny), iz)

    def at_z(dz):
        return (ix, iy, lax.rem(iz + dz + nz, nz))

    barrier = pltpu.get_barrier_semaphore()

    def greet(device):
        pl.semaphore_signal(barrier, inc=1, device_id=device, device_id_type=MESH)

    @pl.loop(1, peers)
    def _(k):
        greet(at_xy(lax.div(k, ny), lax.rem(k, ny)))

    strides = [1, nz - 1, 2, nz - 2] + [CLASSES * k for k in range(1, groups)]
    for dz in strides:
        greet(at_z(dz))

    lane = lax.broadcasted_iota(jnp.int32, (8, 128), 1)
    depth = lax.rem(lane, 32)

    def joined(ref, x):
        return jnp.concatenate([ref[x, y].astype(F32) for y in range(4)], axis=1)

    for x in range(4):
        planes[x] = joined(x_ref, x)

    pl.semaphore_wait(barrier, peers - 1 + len(strides))

    def copy(src, dst, send, recv, device):
        return pltpu.make_async_remote_copy(
            src_ref=src, dst_ref=dst, send_sem=send, recv_sem=recv, device_id=device, device_id_type=MESH
        )

    halo = []
    for h, (dx, dy) in enumerate(HALO):
        first, count = {-1: (0, 1), 0: (0, 4), 1: (3, 1)}[dx]
        halo.append(
            copy(
                planes.at[pl.ds(first, count)], rim.at[h, pl.ds(0, count)],
                halo_s.at[h], halo_r.at[h], at_xy(dx, dy),
            )
        )
        halo[-1].start()
    for one in halo:
        one.wait_recv()

    inside_x = {-1: ix < nx - 1, 0: None, 1: ix > 0}
    inside_y = {-1: iy < ny - 1, 0: None, 1: iy > 0}

    def guarded(value, dx, dy):
        for ok in (inside_x[dx], inside_y[dy]):
            if ok is not None:
                value = jnp.where(ok, value, 0.0)
        return value

    def beside(plane, dy):
        if plane == 0 or plane == 5:
            dx = -1 if plane == 0 else 1
            return guarded(rim[HALO.index((-dx, -dy)), 0], -dx, -dy)
        if dy == 0:
            return planes[plane - 1]
        return guarded(rim[HALO.index((0, -dy)), plane - 1], 0, -dy)

    shifted = {}
    for plane in range(6):
        centre = beside(plane, 0)
        below = jnp.where(lane < 32, pltpu.roll(beside(plane, -1), 32, 1), pltpu.roll(centre, 32, 1))
        above = jnp.where(lane >= 96, pltpu.roll(beside(plane, 1), 96, 1), pltpu.roll(centre, 96, 1))
        for b, value in enumerate((below, centre, above)):
            shifted[plane, b, 0] = jnp.where(depth > 0, pltpu.roll(value, 1, 1), 0.0)
            shifted[plane, b, 1] = value
            shifted[plane, b, 2] = jnp.where(depth < 31, pltpu.roll(value, 127, 1), 0.0)
    rows = []
    for a in range(3):
        for b in range(3):
            for c in range(3):
                rows.append(jnp.concatenate([shifted[x + a, b, c] for x in range(4)], axis=1))
    ones = jnp.where(lax.broadcasted_iota(jnp.int32, (8, 512), 0) == 0, 1.0, 0.0)
    patches = jnp.concatenate(rows + [ones], axis=0).astype(BF16)
    weight = jnp.concatenate([w_ref[...].astype(F32), jnp.zeros((8, chans), F32)], axis=0).astype(BF16)

    partial = lax.dot_general(weight, patches, (((0,), (0,)), ((), ())), preferred_element_type=F32)

    def folded(block):
        return jnp.concatenate([block[:, :256], block[:, 256:]], axis=0)

    for owner in range(nz):
        block = partial[owner * 8 : owner * 8 + 8]
        part[owner % CLASSES, owner // CLASSES] = folded(block).astype(BF16)

    c1, c2, c3 = (lax.rem(cls + s, CLASSES) for s in (1, 2, 3))
    low, high = pl.ds(0, half), pl.ds(half, groups - half)
    stage = [
        copy(part.at[c1], near.at[0], rs1_s.at[0], rs1_r.at[0], at_z(1)),
        copy(part.at[c3], near.at[1], rs1_s.at[1], rs1_r.at[1], at_z(-1)),
        copy(part.at[c2, low], near.at[2, low], rs1_s.at[2], rs1_r.at[2], at_z(2)),
        copy(part.at[c2, high], near.at[2, high], rs1_s.at[3], rs1_r.at[3], at_z(-2)),
    ]
    for one in stage:
        one.start()
    for one in stage:
        one.wait_recv()
    sent = halo + stage
    acc[...] = (
        part[cls].astype(F32) + near[0].astype(F32) + near[1].astype(F32) + near[2].astype(F32)
    ).astype(BF16)

    stage = []
    for k in range(1, groups):
        stage.append(
            copy(
                acc.at[lax.rem(grp + k, groups)], far.at[k - 1],
                rs2_s.at[k - 1], rs2_r.at[k - 1], at_z(CLASSES * k),
            )
        )
        stage[-1].start()
    for one in stage:
        one.wait_recv()
    sent += stage
    pre = acc[grp].astype(F32)
    for k in range(groups - 1):
        pre = pre + far[k].astype(F32)

    square = lax.broadcasted_iota(jnp.int32, (8, 8), 0) == lax.broadcasted_iota(jnp.int32, (8, 8), 1)
    spread = jnp.broadcast_to(bias_ref[...].astype(F32), (8, 8))
    column = jnp.sum(jnp.where(square, spread, 0.0), axis=1, keepdims=True)
    pre = pre + jnp.concatenate([column, column], axis=0)
    sig = jax.nn.sigmoid(pre)
    cot = folded(jnp.concatenate([joined(cot_ref, x) for x in range(4)], axis=1))
    gath[cls, grp] = (cot * sig * (1.0 + pre * (1.0 - sig))).astype(BF16)

    stage = []
    for k in range(1, groups):
        stage.append(
            copy(
                gath.at[cls, grp], gath.at[cls, grp],
                ag1_s.at[k - 1], ag1_r.at[k - 1], at_z(CLASSES * k),
            )
        )
        stage[-1].start()

    act = (pre * sig).astype(BF16)
    for x in range(4):
        for y in range(4):
            first = (x % 2) * 128 + y * 32
            act_ref[x, y] = act[(x // 2) * 8 : (x // 2) * 8 + 8, first : first + 32]

    for one in stage:
        one.wait_recv()
    sent += stage
    stage = [
        copy(gath.at[cls], gath.at[cls], ag2_s.at[0], ag2_r.at[0], at_z(1)),
        copy(gath.at[cls], gath.at[cls], ag2_s.at[1], ag2_r.at[1], at_z(-1)),
        copy(gath.at[cls, low], gath.at[cls, low], ag2_s.at[2], ag2_r.at[2], at_z(2)),
        copy(gath.at[cls, high], gath.at[cls, high], ag2_s.at[3], ag2_r.at[3], at_z(-2)),
    ]
    for one in stage:
        one.start()
    for one in stage:
        one.wait_recv()
    sent += stage

    blocks = []
    for owner in range(nz):
        block = gath[owner % CLASSES, owner // CLASSES].astype(F32)
        blocks.append(jnp.concatenate([block[:8], block[8:]], axis=1))
    slope = jnp.concatenate(blocks, axis=0).astype(BF16)

    product = lax.dot_general(patches, slope, (((1,), (1,)), ((), ())), preferred_element_type=F32)
    size = 256 // peers
    for d in range(peers):
        top = min(max(224 - d * size, 0), size)
        if top:
            grad[d, :top] = product[d * size : d * size + top]
        if top < size:
            grad[d, top:] = jnp.zeros((size - top, chans), F32)

    me = ix * ny + iy

    def scatter(k):
        dx, dy = lax.div(k, ny), lax.rem(k, ny)
        gx, gy, gz = at_xy(dx, dy)
        return copy(grad.at[gx * ny + gy], pieces.at[k - 1], wr_s.at[k - 1], wr_r.at[k - 1], (gx, gy, gz))

    def spread_out(k):
        return copy(
            total.at[me], total.at[me], wa_s.at[k - 1], wa_r.at[k - 1],
            at_xy(lax.div(k, ny), lax.rem(k, ny)),
        )

    @pl.loop(1, peers)
    def _(k):
        scatter(k).start()

    taps = jnp.dot(weight, slope, preferred_element_type=F32)

    def tap_rows(a, b, c, x):
        first = ((a * 3 + b) * 3 + c) * 8
        return taps[first : first + 8, x * 128 : x * 128 + 128]

    own = {}
    for plane in range(6):
        moved = []
        for b in range(3):
            by_depth = []
            for c in range(3):
                terms = [tap_rows(a, b, c, plane - a) for a in range(3) if 0 <= plane - a < 4]
                by_depth.append(functools.reduce(jnp.add, terms))
            moved.append(
                by_depth[1]
                + jnp.where(depth < 31, pltpu.roll(by_depth[0], 127, 1), 0.0)
                + jnp.where(depth > 0, pltpu.roll(by_depth[2], 1, 1), 0.0)
            )
        down, up = pltpu.roll(moved[0], 96, 1), pltpu.roll(moved[2], 32, 1)
        own[plane, 0] = moved[1] + jnp.where(lane < 96, down, 0.0) + jnp.where(lane >= 32, up, 0.0)
        own[plane, -1] = jnp.where(lane >= 96, down, 0.0)
        own[plane, 1] = jnp.where(lane < 32, up, 0.0)

    moves = []
    for h, (dx, dy) in enumerate(HALO):
        if dx == 0:
            for x in range(4):
                back[h, x] = own[x + 1, dy]
        else:
            back[h, 0] = own[0 if dx < 0 else 5, dy]
        count = 4 if dx == 0 else 1
        moves.append(
            copy(
                back.at[h, pl.ds(0, count)], back_in.at[h, pl.ds(0, count)],
                bk_s.at[h], bk_r.at[h], at_xy(dx, dy),
            )
        )
        moves[-1].start()

    @pl.loop(1, peers)
    def _(k):
        scatter(k).wait_recv()

    whole = grad[me]
    for k in range(peers - 1):
        whole = whole + pieces[k]
    total[me] = whole * factor

    @pl.loop(1, peers)
    def _(k):
        spread_out(k).start()

    for one in moves:
        one.wait_recv()
    sums = [own[x + 1, 0] for x in range(4)]
    for h, (dx, dy) in enumerate(HALO):
        if dx == 0:
            for x in range(4):
                sums[x] = sums[x] + guarded(back_in[h, x], dx, dy)
        else:
            x = 3 if dx < 0 else 0
            sums[x] = sums[x] + guarded(back_in[h, 0], dx, dy)
    for x in range(4):
        plane = sums[x].astype(BF16)
        for y in range(4):
            ig_ref[x, y] = plane[:, y * 32 : y * 32 + 32]

    @pl.loop(1, peers)
    def _(k):
        spread_out(k).wait_recv()

    for d in range(peers):
        top = min(max(216 - d * size, 0), size)
        if top:
            wg_ref[d * size : d * size + top] = total[d, :top]
    line = total[216 // size, 216 % size : 216 % size + 1]
    line = jnp.broadcast_to(line, (8, chans))
    own_line = lax.broadcasted_iota(jnp.int32, (8, chans), 1) - iz * 8
    mine = own_line == lax.broadcasted_iota(jnp.int32, (8, chans), 0)
    bg_ref[...] = jnp.sum(jnp.where(mine, line, 0.0), axis=1, keepdims=True)

    for one in sent + moves:
        one.wait_send()

    @pl.loop(1, peers)
    def _(k):
        scatter(k).wait_send()
        spread_out(k).wait_send()


def body(nx, ny, nz, inputs, weight, bias, cotangent):
    groups = nz // CLASSES
    peers = nx * ny
    chans = 8 * nz
    size = 256 // peers
    factor = 1.0 / math.sqrt(512 * peers)
    vmem = pl.BlockSpec(memory_space=pltpu.VMEM)
    sems = [8, 8, 4, 4, groups - 1, groups - 1, groups - 1, groups - 1, 4, 4]
    sems += [peers - 1] * 4 + [8, 8]
    act, grad_in, grad_w, grad_b = pl.pallas_call(
        functools.partial(kernel, nx, ny, nz, factor),
        out_shape=(
            jax.ShapeDtypeStruct((4, 4, 8, 32), BF16),
            jax.ShapeDtypeStruct((4, 4, 8, 32), BF16),
            jax.ShapeDtypeStruct((216, chans), F32),
            jax.ShapeDtypeStruct((8, 1), F32),
        ),
        in_specs=[vmem] * 4,
        out_specs=(vmem,) * 4,
        scratch_shapes=[
            pltpu.VMEM((4, 8, 128), F32),
            pltpu.VMEM((8, 4, 8, 128), F32),
            pltpu.VMEM((CLASSES, groups, 16, 256), BF16),
            pltpu.VMEM((3, groups, 16, 256), BF16),
            pltpu.VMEM((groups, 16, 256), BF16),
            pltpu.VMEM((groups - 1, 16, 256), BF16),
            pltpu.VMEM((CLASSES, groups, 16, 256), BF16),
            pltpu.VMEM((peers, size, chans), F32),
            pltpu.VMEM((peers - 1, size, chans), F32),
            pltpu.VMEM((peers, size, chans), F32),
            pltpu.VMEM((8, 4, 8, 128), F32),
            pltpu.VMEM((8, 4, 8, 128), F32),
        ]
        + [pltpu.SemaphoreType.DMA((n,)) for n in sems],
        compiler_params=pltpu.CompilerParams(collective_id=0, has_side_effects=True),
    )(
        jnp.transpose(inputs, (0, 1, 3, 2)),
        weight.reshape(216, chans),
        bias.reshape(1, 8),
        jnp.transpose(cotangent, (0, 1, 3, 2)),
    )
    return (
        jnp.transpose(act, (0, 1, 3, 2)),
        jnp.transpose(grad_in, (0, 1, 3, 2)),
        grad_w.reshape(3, 3, 3, 8, chans),
        grad_b.reshape(8),
    )


def solution(mesh):
    sizes = (mesh.shape["gx"], mesh.shape["gy"], mesh.shape["ch"])
    return jax.shard_map(
        functools.partial(body, *sizes),
        mesh=mesh,
        in_specs=(
            P("gx", "gy", None, "ch"),
            P(None, None, None, "ch", None),
            P("ch"),
            P("gx", "gy", None, "ch"),
        ),
        out_specs=(
            P("gx", "gy", None, "ch"),
            P("gx", "gy", None, "ch"),
            P(None, None, None, "ch", None),
            P("ch"),
        ),
        check_vma=False,
    )
```

```python
import functools
import math

import jax
import jax.numpy as jnp
from jax import lax
from jax.experimental import pallas as pl
from jax.experimental.pallas import tpu as pltpu
from jax.sharding import PartitionSpec as P

MESH = pl.DeviceIdType.MESH
CLASSES = 4
HALO = [(dx, dy) for dx in (-1, 0, 1) for dy in (-1, 0, 1) if (dx, dy) != (0, 0)]
F32 = jnp.float32
BF16 = jnp.bfloat16


def kernel(
    nx, ny, nz, factor,
    x_hbm, w_hbm, bias_ref, cot_hbm,
    act_hbm, ig_hbm, wg_hbm, bg_ref,
    x_ref, w_ref, cot_ref, act_ref, ig_ref, wg_ref,
    planes, rim, part, near, acc, far, mine, gath, grad, pieces, total, back, back_in,
    local, tokens, halo_s, halo_r, rs1_s, rs1_r, rs2_s, rs2_r, ag1_s, ag1_r, ag2_s, ag2_r,
    wr_s, wr_r, wa_s, wa_r, bk_s, bk_r,
):
    ix, iy, iz = lax.axis_index("gx"), lax.axis_index("gy"), lax.axis_index("ch")
    groups = nz // CLASSES
    half = groups // 2
    peers = nx * ny
    chans = 8 * nz
    cls, grp = lax.rem(iz, CLASSES), lax.div(iz, CLASSES)
    held = lax.rem(cls + 2, CLASSES)

    loads = [
        pltpu.make_async_copy(src, dst, local.at[n])
        for n, (src, dst) in enumerate(((x_hbm, x_ref), (w_hbm, w_ref), (cot_hbm, cot_ref)))
    ]
    for one in loads:
        one.start()

    def at_xy(dx, dy):
        return (lax.rem(ix + dx + nx, nx), lax.rem(iy + dy + ny, ny), iz)

    def at_z(dz):
        return (ix, iy, lax.rem(iz + dz + nz, nz))

    barrier = pltpu.get_barrier_semaphore()

    def greet(device):
        pl.semaphore_signal(barrier, inc=1, device_id=device, device_id_type=MESH)

    strides = [1, -1, 2, -2, 4, -4]
    for dz in strides:
        greet(at_z(dz))

    @pl.loop(1, peers)
    def _(k):
        greet(at_xy(lax.div(k, ny), lax.rem(k, ny)))

    lane = lax.broadcasted_iota(jnp.int32, (8, 128), 1)
    depth = lax.rem(lane, 32)

    def joined(ref, x):
        return jnp.concatenate([ref[x, y].astype(F32) for y in range(4)], axis=1)

    loads[0].wait()
    for x in range(4):
        planes[x] = joined(x_ref, x)

    pl.semaphore_wait(barrier, peers - 1 + len(strides))

    rounds = half - 1

    def pass_tokens():
        for side, dz in enumerate((4, -4)):
            pl.semaphore_signal(tokens.at[side], inc=1, device_id=at_z(dz), device_id_type=MESH)

    if rounds:
        pass_tokens()

    def copy(src, dst, send, recv, device):
        return pltpu.make_async_remote_copy(
            src_ref=src, dst_ref=dst, send_sem=send, recv_sem=recv, device_id=device, device_id_type=MESH
        )

    halo = []
    for h, (dx, dy) in enumerate(HALO):
        first, count = {-1: (0, 1), 0: (0, 4), 1: (3, 1)}[dx]
        halo.append(
            copy(
                planes.at[pl.ds(first, count)], rim.at[h, pl.ds(0, count)],
                halo_s.at[h], halo_r.at[h], at_xy(dx, dy),
            )
        )
        halo[-1].start()
    loads[1].wait()
    weight = jnp.concatenate([w_ref[...].astype(F32), jnp.zeros((8, chans), F32)], axis=0).astype(BF16)
    for one in halo:
        one.wait_recv()

    inside_x = {-1: ix < nx - 1, 0: None, 1: ix > 0}
    inside_y = {-1: iy < ny - 1, 0: None, 1: iy > 0}

    def guarded(value, dx, dy):
        for ok in (inside_x[dx], inside_y[dy]):
            if ok is not None:
                value = jnp.where(ok, value, 0.0)
        return value

    def beside(plane, dy):
        if plane == 0 or plane == 5:
            dx = -1 if plane == 0 else 1
            return guarded(rim[HALO.index((-dx, -dy)), 0], -dx, -dy)
        if dy == 0:
            return planes[plane - 1]
        return guarded(rim[HALO.index((0, -dy)), plane - 1], 0, -dy)

    shifted = {}
    for plane in range(6):
        centre = beside(plane, 0)
        below = jnp.where(lane < 32, pltpu.roll(beside(plane, -1), 32, 1), pltpu.roll(centre, 32, 1))
        above = jnp.where(lane >= 96, pltpu.roll(beside(plane, 1), 96, 1), pltpu.roll(centre, 96, 1))
        for b, value in enumerate((below, centre, above)):
            shifted[plane, b, 0] = jnp.where(depth > 0, pltpu.roll(value, 1, 1), 0.0)
            shifted[plane, b, 1] = value
            shifted[plane, b, 2] = jnp.where(depth < 31, pltpu.roll(value, 127, 1), 0.0)
    rows = []
    for a in range(3):
        for b in range(3):
            for c in range(3):
                rows.append(jnp.concatenate([shifted[x + a, b, c] for x in range(4)], axis=1))
    ones = jnp.where(lax.broadcasted_iota(jnp.int32, (8, 512), 0) == 0, 1.0, 0.0)
    patches = jnp.concatenate(rows + [ones], axis=0).astype(BF16)

    partial = lax.dot_general(weight, patches, (((0,), (0,)), ((), ())), preferred_element_type=F32)

    def folded(block):
        width = block.shape[1] // 2
        return jnp.concatenate([block[:, :width], block[:, width:]], axis=0)

    for owner in range(nz):
        block = partial[owner * 8 : owner * 8 + 8]
        part[owner % CLASSES, owner // CLASSES] = folded(block).astype(BF16)

    order = sorted(range(-half, half), key=lambda j: -abs(4 * j + 2))
    batches = [order[:half], order[half:]] if half > 1 else [order]
    sources = [(1, None), (-1, None), (2, range(0, half)), (-2, range(1 - half, 1))]

    def owner_group(device, j):
        return lax.div(lax.rem(iz + device + 4 * j + 2 + nz, nz), CLASSES)

    near_sent = []
    for n, batch in enumerate(batches):
        for j in batch:
            for s, (dz, members) in enumerate(sources):
                if members is None or j in members:
                    kind = lax.rem(cls + dz + 2 + CLASSES, CLASSES)
                    one = copy(
                        part.at[kind, owner_group(dz, j)], near.at[s, j + half],
                        rs1_s.at[s, n], rs1_r.at[s, n], at_z(dz),
                    )
                    one.start()
                    near_sent.append(one)

    for r in range(rounds):
        for side in range(2):
            pl.semaphore_wait(tokens.at[side], 1)
        if r < rounds - 1:
            pass_tokens()

    sent = list(halo)
    counts = {}
    for n, batch in enumerate(batches):
        for s, (dz, members) in enumerate(sources):
            counts[s, n] = len([j for j in batch if members is None or j in members])
            if counts[s, n]:
                span = near.at[s, pl.ds(0, counts[s, n])]
                copy(span, span, rs1_s.at[s, n], rs1_r.at[s, n], at_z(dz)).wait_recv()
        for j in batch:
            value = part[held, owner_group(0, j)].astype(F32)
            for s, (dz, members) in enumerate(sources):
                if members is None or j in members:
                    value = value + near[s, j + half].astype(F32)
            acc[j + half] = value.astype(BF16)
            one = copy(
                acc.at[j + half], far.at[j + half], rs2_s.at[j + half], rs2_r.at[j + half], at_z(4 * j + 2)
            )
            one.start()
            sent.append(one)

    square = lax.broadcasted_iota(jnp.int32, (8, 8), 0) == lax.broadcasted_iota(jnp.int32, (8, 8), 1)
    spread = jnp.broadcast_to(bias_ref[...].astype(F32), (8, 8))
    column = jnp.sum(jnp.where(square, spread, 0.0), axis=1, keepdims=True)
    pre = jnp.concatenate([column, column], axis=0)
    loads[2].wait()
    cot = folded(jnp.concatenate([joined(cot_ref, x) for x in range(4)], axis=1))
    for j in reversed(order):
        copy(
            acc.at[j + half], far.at[j + half], rs2_s.at[j + half], rs2_r.at[j + half], at_z(4 * j + 2)
        ).wait_recv()
        pre = pre + far[j + half].astype(F32)
    sig = jax.nn.sigmoid(pre)
    mine[...] = (cot * sig * (1.0 + pre * (1.0 - sig))).astype(BF16)

    for j in order:
        one = copy(mine, gath.at[cls, grp], ag1_s.at[j + half], ag1_r.at[j + half], at_z(4 * j + 2))
        one.start()
        sent.append(one)

    act = (pre * sig).astype(BF16)
    for x in range(4):
        for y in range(4):
            first = (x % 2) * 128 + y * 32
            act_ref[x, y] = act[(x // 2) * 8 : (x // 2) * 8 + 8, first : first + 32]
    stores = [pltpu.make_async_copy(act_ref, act_hbm, local.at[3])]
    stores[0].start()

    for j in reversed(order):
        slot = gath.at[held, owner_group(0, -j - 1)]
        copy(mine, slot, ag1_s.at[j + half], ag1_r.at[j + half], at_z(4 * j + 2)).wait_recv()
        for s, (dz, members) in enumerate(sources):
            if members is None or j in members:
                copy(slot, slot, ag2_s.at[s], ag2_r.at[s], at_z(dz)).start()
    for s, (dz, members) in enumerate(sources):
        span = gath.at[0] if members is None else gath.at[0, pl.ds(0, half)]
        copy(span, span, ag2_s.at[s], ag2_r.at[s], at_z(dz)).wait_recv()

    blocks = []
    for owner in range(nz):
        block = gath[owner % CLASSES, owner // CLASSES].astype(F32)
        blocks.append(jnp.concatenate([block[:8], block[8:]], axis=1))
    slope = jnp.concatenate(blocks, axis=0).astype(BF16)

    product = lax.dot_general(patches, slope, (((1,), (1,)), ((), ())), preferred_element_type=F32)
    size = 256 // peers
    for d in range(peers):
        top = min(max(224 - d * size, 0), size)
        lines = [product[d * size : d * size + top]] if top else []
        if top < size:
            lines.append(jnp.zeros((size - top, chans), F32))
        grad[d] = folded(jnp.concatenate(lines, axis=0)).astype(BF16)

    me = ix * ny + iy

    def scatter(k):
        gx, gy, gz = at_xy(lax.div(k, ny), lax.rem(k, ny))
        return copy(grad.at[gx * ny + gy], pieces.at[k - 1], wr_s.at[k - 1], wr_r.at[k - 1], (gx, gy, gz))

    def spread_out(k):
        return copy(
            total.at[me], total.at[me], wa_s.at[k - 1], wa_r.at[k - 1],
            at_xy(lax.div(k, ny), lax.rem(k, ny)),
        )

    @pl.loop(1, peers)
    def _(k):
        scatter(k).start()

    taps = jnp.dot(weight, slope, preferred_element_type=F32)

    def tap_rows(a, b, c, x):
        first = ((a * 3 + b) * 3 + c) * 8
        return taps[first : first + 8, x * 128 : x * 128 + 128]

    own = {}
    for plane in range(6):
        moved = []
        for b in range(3):
            by_depth = []
            for c in range(3):
                terms = [tap_rows(a, b, c, plane - a) for a in range(3) if 0 <= plane - a < 4]
                by_depth.append(functools.reduce(jnp.add, terms))
            moved.append(
                by_depth[1]
                + jnp.where(depth < 31, pltpu.roll(by_depth[0], 127, 1), 0.0)
                + jnp.where(depth > 0, pltpu.roll(by_depth[2], 1, 1), 0.0)
            )
        down, up = pltpu.roll(moved[0], 96, 1), pltpu.roll(moved[2], 32, 1)
        own[plane, 0] = moved[1] + jnp.where(lane < 96, down, 0.0) + jnp.where(lane >= 32, up, 0.0)
        own[plane, -1] = jnp.where(lane >= 96, down, 0.0)
        own[plane, 1] = jnp.where(lane < 32, up, 0.0)

    moves = []
    for h, (dx, dy) in enumerate(HALO):
        if dx == 0:
            for x in range(4):
                back[h, x] = own[x + 1, dy]
        else:
            back[h, 0] = own[0 if dx < 0 else 5, dy]
        count = 4 if dx == 0 else 1
        moves.append(
            copy(
                back.at[h, pl.ds(0, count)], back_in.at[h, pl.ds(0, count)],
                bk_s.at[h], bk_r.at[h], at_xy(dx, dy),
            )
        )
        moves[-1].start()

    @pl.loop(1, peers)
    def _(k):
        scatter(k).wait_recv()

    whole = grad[me].astype(F32)
    for k in range(peers - 1):
        whole = whole + pieces[k].astype(F32)
    total[me] = (whole * factor).astype(BF16)

    @pl.loop(1, peers)
    def _(k):
        spread_out(k).start()

    for one in moves:
        one.wait_recv()
    sums = [own[x + 1, 0] for x in range(4)]
    for h, (dx, dy) in enumerate(HALO):
        if dx == 0:
            for x in range(4):
                sums[x] = sums[x] + guarded(back_in[h, x], dx, dy)
        else:
            x = 3 if dx < 0 else 0
            sums[x] = sums[x] + guarded(back_in[h, 0], dx, dy)
    for x in range(4):
        plane = sums[x].astype(BF16)
        for y in range(4):
            ig_ref[x, y] = plane[:, y * 32 : y * 32 + 32]
    stores.append(pltpu.make_async_copy(ig_ref, ig_hbm, local.at[4]))
    stores[1].start()

    for one in sent + moves:
        one.wait_send()
    for (s, n), count in counts.items():
        if count:
            span = near.at[s, pl.ds(0, count)]
            copy(span, span, rs1_s.at[s, n], rs1_r.at[s, n], at_z(1)).wait_send()
    for s, (dz, members) in enumerate(sources):
        span = gath.at[0] if members is None else gath.at[0, pl.ds(0, half)]
        copy(span, span, ag2_s.at[s], ag2_r.at[s], at_z(dz)).wait_send()

    @pl.loop(1, peers)
    def _(k):
        scatter(k).wait_send()

    @pl.loop(1, peers)
    def _(k):
        spread_out(k).wait_recv()

    def chunk(d):
        value = total[d].astype(F32)
        return jnp.concatenate([value[:size], value[size:]], axis=1)

    for d in range(peers):
        top = min(max(216 - d * size, 0), size)
        if top:
            wg_ref[d * size : d * size + top] = chunk(d)[:top]
    stores.append(pltpu.make_async_copy(wg_ref, wg_hbm, local.at[5]))
    stores[2].start()
    line = chunk(216 // size)[216 % size : 216 % size + 1]
    line = jnp.broadcast_to(line, (8, chans))
    own_line = lax.broadcasted_iota(jnp.int32, (8, chans), 1) - iz * 8
    mine_line = own_line == lax.broadcasted_iota(jnp.int32, (8, chans), 0)
    column = jnp.sum(jnp.where(mine_line, line, 0.0), axis=1, keepdims=True)
    bg_ref[...] = jnp.sum(jnp.where(square, jnp.broadcast_to(column, (8, 8)), 0.0), axis=0, keepdims=True)

    @pl.loop(1, peers)
    def _(k):
        spread_out(k).wait_send()

    for one in stores:
        one.wait()


def hand_on(*refs):
    for source, target in zip(refs[:4], refs[4:]):
        target[...] = source[...]


def body(nx, ny, nz, inputs, weight, bias, cotangent):
    groups = nz // CLASSES
    half = groups // 2
    peers = nx * ny
    chans = 8 * nz
    size = 256 // peers
    factor = 1.0 / math.sqrt(512 * peers)
    vmem = pl.BlockSpec(memory_space=pltpu.VMEM)
    hbm = pl.BlockSpec(memory_space=pl.ANY)
    sems = [(6,)] + [(8,)] * 2 + [(4, 2)] * 2 + [(groups,)] * 4 + [(4,)] * 2 + [(peers - 1,)] * 4 + [(8,)] * 2
    sems = [pltpu.SemaphoreType.DMA(n) for n in sems]
    shapes = (
        jax.ShapeDtypeStruct((4, 4, 8, 32), BF16),
        jax.ShapeDtypeStruct((4, 4, 8, 32), BF16),
        jax.ShapeDtypeStruct((216, chans), F32),
        jax.ShapeDtypeStruct((1, 8), F32),
    )
    results = pl.pallas_call(
        functools.partial(kernel, nx, ny, nz, factor),
        out_shape=shapes,
        in_specs=[hbm, hbm, vmem, hbm],
        out_specs=(hbm, hbm, hbm, vmem),
        scratch_shapes=[
            pltpu.VMEM((4, 4, 8, 32), BF16),
            pltpu.VMEM((216, chans), BF16),
            pltpu.VMEM((4, 4, 8, 32), BF16),
            pltpu.VMEM((4, 4, 8, 32), BF16),
            pltpu.VMEM((4, 4, 8, 32), BF16),
            pltpu.VMEM((216, chans), F32),
            pltpu.VMEM((4, 8, 128), F32),
            pltpu.VMEM((8, 4, 8, 128), F32),
            pltpu.VMEM((CLASSES, groups, 16, 256), BF16),
            pltpu.VMEM((4, groups, 16, 256), BF16),
            pltpu.VMEM((groups, 16, 256), BF16),
            pltpu.VMEM((groups, 16, 256), BF16),
            pltpu.VMEM((16, 256), BF16),
            pltpu.VMEM((CLASSES, groups, 16, 256), BF16),
            pltpu.VMEM((peers, 2 * size, chans // 2), BF16),
            pltpu.VMEM((peers - 1, 2 * size, chans // 2), BF16),
            pltpu.VMEM((peers, 2 * size, chans // 2), BF16),
            pltpu.VMEM((8, 4, 8, 128), F32),
            pltpu.VMEM((8, 4, 8, 128), F32),
            sems[0],
            pltpu.SemaphoreType.REGULAR((2,)),
        ]
        + sems[1:],
        compiler_params=pltpu.CompilerParams(collective_id=0, has_side_effects=True),
    )(
        jnp.transpose(inputs, (0, 1, 3, 2)),
        weight.reshape(216, chans),
        bias.reshape(1, 8),
        jnp.transpose(cotangent, (0, 1, 3, 2)),
    )
    act, grad_in, grad_w, grad_b = pl.pallas_call(
        hand_on,
        out_shape=shapes,
        in_specs=[vmem] * 4,
        out_specs=(vmem,) * 4,
    )(*results)
    return (
        jnp.transpose(act, (0, 1, 3, 2)),
        jnp.transpose(grad_in, (0, 1, 3, 2)),
        grad_w.reshape(3, 3, 3, 8, chans),
        grad_b.reshape(8),
    )


def solution(mesh):
    sizes = (mesh.shape["gx"], mesh.shape["gy"], mesh.shape["ch"])
    return jax.shard_map(
        functools.partial(body, *sizes),
        mesh=mesh,
        in_specs=(
            P("gx", "gy", None, "ch"),
            P(None, None, None, "ch", None),
            P("ch"),
            P("gx", "gy", None, "ch"),
        ),
        out_specs=(
            P("gx", "gy", None, "ch"),
            P("gx", "gy", None, "ch"),
            P(None, None, None, "ch", None),
            P("ch"),
        ),
        check_vma=False,
    )
```

```python
import functools
import math

import jax
import jax.numpy as jnp
from jax import lax
from jax.experimental import pallas as pl
from jax.experimental.pallas import tpu as pltpu
from jax.sharding import PartitionSpec as P

MESH = pl.DeviceIdType.MESH
CLASSES = 4
HALO = [(dx, dy) for dx in (-1, 0, 1) for dy in (-1, 0, 1) if (dx, dy) != (0, 0)]
F32 = jnp.float32
BF16 = jnp.bfloat16


def kernel(
    nx, ny, nz, factor,
    x_hbm, w_hbm, bias_hbm, cot_hbm,
    act_hbm, ig_hbm, total,
    x_ref, w_ref, bias_ref, cot_ref, act_ref, ig_ref,
    planes, rim, part, near, acc, relay, far, mine, gath, grad, pieces, chunk, back, back_in,
    local, tokens, halo_s, halo_r, rs1_s, rs1_r, rl_s, rl_r, rs2_s, rs2_r, ag1_s, ag1_r, ag2_s, ag2_r,
    wr_s, wr_r, wa_s, wa_r, bk_s, bk_r,
):
    ix, iy, iz = lax.axis_index("gx"), lax.axis_index("gy"), lax.axis_index("ch")
    groups = nz // CLASSES
    half = groups // 2
    quarter = half // 2
    peers = nx * ny
    chans = 8 * nz
    cls, grp = lax.rem(iz, CLASSES), lax.div(iz, CLASSES)
    held = lax.rem(cls + 2, CLASSES)

    loads = [
        pltpu.make_async_copy(src, dst, local.at[n])
        for n, (src, dst) in enumerate(((x_hbm, x_ref), (w_hbm, w_ref), (cot_hbm, cot_ref), (bias_hbm, bias_ref)))
    ]
    for one in loads:
        one.start()

    def at_xy(dx, dy):
        return (lax.rem(ix + dx + nx, nx), lax.rem(iy + dy + ny, ny), iz)

    def at_z(dz):
        return (ix, iy, lax.rem(iz + dz + nz, nz))

    barrier = pltpu.get_barrier_semaphore()

    def greet(device):
        pl.semaphore_signal(barrier, inc=1, device_id=device, device_id_type=MESH)

    for dz in (1, -1, 2, -2):
        greet(at_z(dz))
    for dx, dy in HALO:
        greet(at_xy(dx, dy))

    lane = lax.broadcasted_iota(jnp.int32, (8, 128), 1)
    depth = lax.rem(lane, 32)

    def joined(ref, x):
        return jnp.concatenate([ref[x, y].astype(F32) for y in range(4)], axis=1)

    loads[0].wait()
    for x in range(4):
        planes[x] = joined(x_ref, x)

    pl.semaphore_wait(barrier, 4 + len(HALO))

    def pass_token(n, device):
        pl.semaphore_signal(tokens.at[n], inc=1, device_id=device, device_id_type=MESH)

    def await_tokens(*ns):
        for n in ns:
            pl.semaphore_wait(tokens.at[n], 1)

    if quarter:
        pass_token(0, at_z(2))
        pass_token(1, at_z(-2))

    def copy(src, dst, send, recv, device):
        return pltpu.make_async_remote_copy(
            src_ref=src, dst_ref=dst, send_sem=send, recv_sem=recv, device_id=device, device_id_type=MESH
        )

    halo = []
    for h, (dx, dy) in enumerate(HALO):
        first, count = {-1: (0, 1), 0: (0, 4), 1: (3, 1)}[dx]
        halo.append(
            copy(
                planes.at[pl.ds(first, count)], rim.at[h, pl.ds(0, count)],
                halo_s.at[h], halo_r.at[h], at_xy(dx, dy),
            )
        )
        halo[-1].start()
    loads[1].wait()
    weight = jnp.concatenate([w_ref[...].astype(F32), jnp.zeros((8, chans), F32)], axis=0).astype(BF16)
    for one in halo:
        one.wait_recv()
    if ny > 4:
        pass_token(4, at_xy(0, 2))
        pass_token(5, at_xy(0, -2))
    if quarter:
        await_tokens(0, 1)
        pass_token(2, at_z(4))
        pass_token(3, at_z(-4))

    inside_x = {-1: ix < nx - 1, 0: None, 1: ix > 0}
    inside_y = {-1: iy < ny - 1, 0: None, 1: iy > 0}

    def guarded(value, dx, dy):
        for ok in (inside_x[dx], inside_y[dy]):
            if ok is not None:
                value = jnp.where(ok, value, 0.0)
        return value

    def beside(plane, dy):
        if plane == 0 or plane == 5:
            dx = -1 if plane == 0 else 1
            return guarded(rim[HALO.index((-dx, -dy)), 0], -dx, -dy)
        if dy == 0:
            return planes[plane - 1]
        return guarded(rim[HALO.index((0, -dy)), plane - 1], 0, -dy)

    shifted = {}
    for plane in range(6):
        centre = beside(plane, 0)
        below = jnp.where(lane < 32, pltpu.roll(beside(plane, -1), 32, 1), pltpu.roll(centre, 32, 1))
        above = jnp.where(lane >= 96, pltpu.roll(beside(plane, 1), 96, 1), pltpu.roll(centre, 96, 1))
        for b, value in enumerate((below, centre, above)):
            shifted[plane, b, 0] = jnp.where(depth > 0, pltpu.roll(value, 1, 1), 0.0)
            shifted[plane, b, 1] = value
            shifted[plane, b, 2] = jnp.where(depth < 31, pltpu.roll(value, 127, 1), 0.0)
    rows = []
    for a in range(3):
        for b in range(3):
            for c in range(3):
                rows.append(jnp.concatenate([shifted[x + a, b, c] for x in range(4)], axis=1))
    ones = jnp.where(lax.broadcasted_iota(jnp.int32, (8, 512), 0) == 0, 1.0, 0.0)
    patches = jnp.concatenate(rows + [ones], axis=0).astype(BF16)

    partial = lax.dot_general(weight, patches, (((0,), (0,)), ((), ())), preferred_element_type=F32)

    def folded(block):
        width = block.shape[1] // 2
        return jnp.concatenate([block[:, :width], block[:, width:]], axis=0)

    for owner in range(nz):
        block = partial[owner * 8 : owner * 8 + 8]
        part[owner % CLASSES, owner // CLASSES] = folded(block).astype(BF16)

    order = sorted(range(-half, half), key=lambda j: -abs(4 * j + 2))
    outer, inner = order[: 2 * quarter], order[2 * quarter :]
    batches = [outer, inner]
    sources = [(1, None), (-1, None), (2, range(0, half)), (-2, range(1 - half, 1))]

    def owner_group(device, j):
        return lax.div(lax.rem(iz + device + 4 * j + 2 + nz, nz), CLASSES)

    near_sent = []
    for n, batch in enumerate(batches):
        for j in batch:
            for s, (dz, members) in enumerate(sources):
                if members is None or j in members:
                    kind = lax.rem(cls + dz + 2 + CLASSES, CLASSES)
                    one = copy(
                        part.at[kind, owner_group(dz, j)], near.at[s, j + half],
                        rs1_s.at[s, n], rs1_r.at[s, n], at_z(dz),
                    )
                    one.start()
                    near_sent.append(one)

    if quarter:
        await_tokens(2, 3)

    sent = list(halo)
    counts = {}
    relays = {}
    for n, batch in enumerate(batches):
        for s, (dz, members) in enumerate(sources):
            counts[s, n] = len([j for j in batch if members is None or j in members])
            if counts[s, n]:
                span = near.at[s, pl.ds(0, counts[s, n])]
                copy(span, span, rs1_s.at[s, n], rs1_r.at[s, n], at_z(dz)).wait_recv()
        for j in batch:
            value = part[held, owner_group(0, j)].astype(F32)
            for s, (dz, members) in enumerate(sources):
                if members is None or j in members:
                    value = value + near[s, j + half].astype(F32)
            acc[j + half] = value.astype(BF16)
            if j in outer:
                step = quarter if j > 0 else -quarter
                slot = j - step + half
                one = copy(acc.at[j + half], relay.at[slot], rl_s.at[slot], rl_r.at[slot], at_z(4 * step))
                one.start()
                relays[j - step] = one

    far_in = []
    for j in inner:
        if quarter:
            relays[j].wait()
            acc[j + half] = (acc[j + half].astype(F32) + relay[j + half].astype(F32)).astype(BF16)
        one = copy(acc.at[j + half], far.at[j + half], rs2_s.at[j + half], rs2_r.at[j + half], at_z(4 * j + 2))
        one.start()
        far_in.insert(0, (j, one))
        sent.append(one)

    square = lax.broadcasted_iota(jnp.int32, (8, 8), 0) == lax.broadcasted_iota(jnp.int32, (8, 8), 1)
    loads[3].wait()
    spread = jnp.broadcast_to(bias_ref[...].astype(F32), (8, 8))
    column = jnp.sum(jnp.where(square, spread, 0.0), axis=1, keepdims=True)
    pre = jnp.concatenate([column, column], axis=0)
    loads[2].wait()
    cot = folded(jnp.concatenate([joined(cot_ref, x) for x in range(4)], axis=1))
    for j, one in far_in:
        one.wait_recv()
        pre = pre + far[j + half].astype(F32)
    sig = jax.nn.sigmoid(pre)
    mine[...] = (cot * sig * (1.0 + pre * (1.0 - sig))).astype(BF16)

    for j in order:
        one = copy(mine, gath.at[cls, grp], ag1_s.at[j + half], ag1_r.at[j + half], at_z(4 * j + 2))
        one.start()
        sent.append(one)

    act = (pre * sig).astype(BF16)
    for x in range(4):
        for y in range(4):
            first = (x % 2) * 128 + y * 32
            act_ref[x, y] = act[(x // 2) * 8 : (x // 2) * 8 + 8, first : first + 32]
    stores = [pltpu.make_async_copy(act_ref, act_hbm, local.at[3])]
    stores[0].start()

    for j in reversed(order):
        slot = gath.at[held, owner_group(0, -j - 1)]
        copy(mine, slot, ag1_s.at[j + half], ag1_r.at[j + half], at_z(4 * j + 2)).wait_recv()
        for s, (dz, members) in enumerate(sources):
            if members is None or j in members:
                copy(slot, slot, ag2_s.at[s], ag2_r.at[s], at_z(dz)).start()
    for s, (dz, members) in enumerate(sources):
        span = gath.at[0] if members is None else gath.at[0, pl.ds(0, half)]
        copy(span, span, ag2_s.at[s], ag2_r.at[s], at_z(dz)).wait_recv()

    blocks = []
    for owner in range(nz):
        block = gath[owner % CLASSES, owner // CLASSES].astype(F32)
        blocks.append(jnp.concatenate([block[:8], block[8:]], axis=1))
    slope = jnp.concatenate(blocks, axis=0).astype(BF16)

    product = lax.dot_general(patches, slope, (((1,), (1,)), ((), ())), preferred_element_type=F32)
    size = 256 // peers
    for d in range(peers):
        top = min(max(224 - d * size, 0), size)
        lines = [product[d * size : d * size + top]] if top else []
        if top < size:
            lines.append(jnp.zeros((size - top, chans), F32))
        grad[d] = folded(jnp.concatenate(lines, axis=0)).astype(BF16)

    me = ix * ny + iy

    others = [(dx, dy) for dx in range(nx) for dy in range(ny) if (dx, dy) != (0, 0)]
    others.sort(key=lambda d: -(min(d[0], nx - d[0]) + (min(d[1], ny - d[1]) + 1) // 2))
    if ny > 4:
        await_tokens(4, 5)
    for n, (dx, dy) in enumerate(others):
        gx, gy, gz = at_xy(dx, dy)
        copy(grad.at[gx * ny + gy], pieces.at[n], wr_s, wr_r, (gx, gy, gz)).start()

    taps = jnp.dot(weight, slope, preferred_element_type=F32)

    def tap_rows(a, b, c, x):
        first = ((a * 3 + b) * 3 + c) * 8
        return taps[first : first + 8, x * 128 : x * 128 + 128]

    own = {}
    for plane in range(6):
        moved = []
        for b in range(3):
            by_depth = []
            for c in range(3):
                terms = [tap_rows(a, b, c, plane - a) for a in range(3) if 0 <= plane - a < 4]
                by_depth.append(functools.reduce(jnp.add, terms))
            moved.append(
                by_depth[1]
                + jnp.where(depth < 31, pltpu.roll(by_depth[0], 127, 1), 0.0)
                + jnp.where(depth > 0, pltpu.roll(by_depth[2], 1, 1), 0.0)
            )
        down, up = pltpu.roll(moved[0], 96, 1), pltpu.roll(moved[2], 32, 1)
        own[plane, 0] = moved[1] + jnp.where(lane < 96, down, 0.0) + jnp.where(lane >= 32, up, 0.0)
        own[plane, -1] = jnp.where(lane >= 96, down, 0.0)
        own[plane, 1] = jnp.where(lane < 32, up, 0.0)

    moves = []
    for h, (dx, dy) in enumerate(HALO):
        if dx == 0:
            for x in range(4):
                back[h, x] = own[x + 1, dy]
        else:
            back[h, 0] = own[0 if dx < 0 else 5, dy]
        count = 4 if dx == 0 else 1
        moves.append(
            copy(
                back.at[h, pl.ds(0, count)], back_in.at[h, pl.ds(0, count)],
                bk_s.at[h], bk_r.at[h], at_xy(dx, dy),
            )
        )
        moves[-1].start()

    copy(pieces, pieces, wr_s, wr_r, at_xy(0, 1)).wait_recv()
    whole = grad[me].astype(F32)
    for k in range(peers - 1):
        whole = whole + pieces[k].astype(F32)
    chunk[...] = (whole * factor).astype(BF16)
    for dx, dy in others:
        copy(chunk, total.at[me], wa_s, wa_r, at_xy(dx, dy)).start()
    stores.append(pltpu.make_async_copy(chunk, total.at[me], local.at[5]))
    stores[-1].start()

    for one in moves:
        one.wait_recv()
    sums = [own[x + 1, 0] for x in range(4)]
    for h, (dx, dy) in enumerate(HALO):
        if dx == 0:
            for x in range(4):
                sums[x] = sums[x] + guarded(back_in[h, x], dx, dy)
        else:
            x = 3 if dx < 0 else 0
            sums[x] = sums[x] + guarded(back_in[h, 0], dx, dy)
    for x in range(4):
        plane = sums[x].astype(BF16)
        for y in range(4):
            ig_ref[x, y] = plane[:, y * 32 : y * 32 + 32]
    stores.append(pltpu.make_async_copy(ig_ref, ig_hbm, local.at[4]))
    stores[-1].start()

    for one in sent + moves:
        one.wait_send()
    for (s, n), count in counts.items():
        if count:
            span = near.at[s, pl.ds(0, count)]
            copy(span, span, rs1_s.at[s, n], rs1_r.at[s, n], at_z(1)).wait_send()
    for s, (dz, members) in enumerate(sources):
        span = gath.at[0] if members is None else gath.at[0, pl.ds(0, half)]
        copy(span, span, ag2_s.at[s], ag2_r.at[s], at_z(dz)).wait_send()

    rest = total.at[pl.ds(0, peers - 1)]
    copy(pieces, pieces, wr_s, wr_r, at_xy(0, 1)).wait_send()
    copy(rest, rest, wa_s, wa_r, at_xy(0, 1)).wait()
    for one in stores:
        one.wait()


def hand_on(size, act_in, ig_in, total, act, ig, wg, bg):
    chans = wg.shape[1]
    act[...] = act_in[...]
    ig[...] = ig_in[...]

    def chunk(d):
        value = total[d].astype(F32)
        return jnp.concatenate([value[:size], value[size:]], axis=1)

    for d in range(total.shape[0]):
        top = min(max(216 - d * size, 0), size)
        if top:
            wg[d * size : d * size + top] = chunk(d)[:top]
    line = jnp.broadcast_to(chunk(216 // size)[216 % size : 216 % size + 1], (8, chans))
    lane = lax.broadcasted_iota(jnp.int32, (8, chans), 1) - lax.axis_index("ch") * 8
    column = jnp.where(lane == lax.broadcasted_iota(jnp.int32, (8, chans), 0), line, 0.0)
    column = jnp.broadcast_to(jnp.sum(column, axis=1, keepdims=True), (8, 8))
    square = lax.broadcasted_iota(jnp.int32, (8, 8), 0) == lax.broadcasted_iota(jnp.int32, (8, 8), 1)
    bg[...] = jnp.sum(jnp.where(square, column, 0.0), axis=0, keepdims=True)


def body(nx, ny, nz, inputs, weight, bias, cotangent):
    groups = nz // CLASSES
    half = groups // 2
    peers = nx * ny
    chans = 8 * nz
    size = 256 // peers
    factor = 1.0 / math.sqrt(512 * peers)
    vmem = pl.BlockSpec(memory_space=pltpu.VMEM)
    hbm = pl.BlockSpec(memory_space=pl.ANY)
    sems = [(8,)] * 2 + [(4, 2)] * 2 + [(groups,)] * 6 + [(4,)] * 2 + [()] * 4 + [(8,)] * 2
    cells = jax.ShapeDtypeStruct((4, 4, 8, 32), BF16)
    gathered = jax.ShapeDtypeStruct((peers, 2 * size, chans // 2), BF16)
    results = pl.pallas_call(
        functools.partial(kernel, nx, ny, nz, factor),
        out_shape=(cells, cells, gathered),
        in_specs=[hbm] * 4,
        out_specs=(hbm,) * 3,
        scratch_shapes=[
            pltpu.VMEM((4, 4, 8, 32), BF16),
            pltpu.VMEM((216, chans), BF16),
            pltpu.VMEM((1, 8), BF16),
            pltpu.VMEM((4, 4, 8, 32), BF16),
            pltpu.VMEM((4, 4, 8, 32), BF16),
            pltpu.VMEM((4, 4, 8, 32), BF16),
            pltpu.VMEM((4, 8, 128), F32),
            pltpu.VMEM((8, 4, 8, 128), F32),
            pltpu.VMEM((CLASSES, groups, 16, 256), BF16),
            pltpu.VMEM((4, groups, 16, 256), BF16),
            pltpu.VMEM((groups, 16, 256), BF16),
            pltpu.VMEM((groups, 16, 256), BF16),
            pltpu.VMEM((groups, 16, 256), BF16),
            pltpu.VMEM((16, 256), BF16),
            pltpu.VMEM((CLASSES, groups, 16, 256), BF16),
            pltpu.VMEM((peers, 2 * size, chans // 2), BF16),
            pltpu.VMEM((peers - 1, 2 * size, chans // 2), BF16),
            pltpu.VMEM((2 * size, chans // 2), BF16),
            pltpu.VMEM((8, 4, 8, 128), F32),
            pltpu.VMEM((8, 4, 8, 128), F32),
            pltpu.SemaphoreType.DMA((6,)),
            pltpu.SemaphoreType.REGULAR((6,)),
        ]
        + [pltpu.SemaphoreType.DMA(n) for n in sems],
        compiler_params=pltpu.CompilerParams(collective_id=0, has_side_effects=True),
    )(
        jnp.transpose(inputs, (0, 1, 3, 2)),
        weight.reshape(216, chans),
        bias.reshape(1, 8),
        jnp.transpose(cotangent, (0, 1, 3, 2)),
    )
    act, grad_in, grad_w, grad_b = pl.pallas_call(
        functools.partial(hand_on, size),
        out_shape=(cells, cells, jax.ShapeDtypeStruct((216, chans), F32), jax.ShapeDtypeStruct((1, 8), F32)),
        in_specs=[vmem] * 3,
        out_specs=(vmem,) * 4,
    )(*results)
    return (
        jnp.transpose(act, (0, 1, 3, 2)),
        jnp.transpose(grad_in, (0, 1, 3, 2)),
        grad_w.reshape(3, 3, 3, 8, chans),
        grad_b.reshape(8),
    )


def solution(mesh):
    sizes = (mesh.shape["gx"], mesh.shape["gy"], mesh.shape["ch"])
    return jax.shard_map(
        functools.partial(body, *sizes),
        mesh=mesh,
        in_specs=(
            P("gx", "gy", None, "ch"),
            P(None, None, None, "ch", None),
            P("ch"),
            P("gx", "gy", None, "ch"),
        ),
        out_specs=(
            P("gx", "gy", None, "ch"),
            P("gx", "gy", None, "ch"),
            P(None, None, None, "ch", None),
            P("ch"),
        ),
        check_vma=False,
    )
```

```python
import functools
import math

import jax
import jax.numpy as jnp
from jax import lax
from jax.experimental import pallas as pl
from jax.experimental.pallas import tpu as pltpu
from jax.sharding import PartitionSpec as P

MESH = pl.DeviceIdType.MESH
CLASSES = 4
HALO = [(dx, dy) for dx in (-1, 0, 1) for dy in (-1, 0, 1) if (dx, dy) != (0, 0)]
F32 = jnp.float32
BF16 = jnp.bfloat16


def kernel(
    nx, ny, nz, factor,
    x_hbm, w_hbm, bias_hbm, cot_hbm,
    act_hbm, ig_hbm, total,
    x_ref, w_ref, bias_ref, cot_ref, act_ref, ig_ref,
    planes, rim, part, near, acc, far, mine, gath, grad, pieces, chunk, back, back_in,
    local, tokens, halo_s, halo_r, rs1_s, rs1_r, rs2_s, rs2_r, ag1_s, ag1_r, ag2_s, ag2_r,
    wr_s, wr_r, wa_s, wa_r, bk_s, bk_r,
):
    ix, iy, iz = lax.axis_index("gx"), lax.axis_index("gy"), lax.axis_index("ch")
    groups = nz // CLASSES
    half = groups // 2
    quarter = half // 2
    peers = nx * ny
    chans = 8 * nz
    cls, grp = lax.rem(iz, CLASSES), lax.div(iz, CLASSES)
    held = lax.rem(cls + 2, CLASSES)

    loads = [
        pltpu.make_async_copy(src, dst, local.at[n])
        for n, (src, dst) in enumerate(((x_hbm, x_ref), (w_hbm, w_ref), (cot_hbm, cot_ref), (bias_hbm, bias_ref)))
    ]
    for one in loads:
        one.start()

    def at_xy(dx, dy):
        return (lax.rem(ix + dx + nx, nx), lax.rem(iy + dy + ny, ny), iz)

    def at_z(dz):
        return (ix, iy, lax.rem(iz + dz + nz, nz))

    barrier = pltpu.get_barrier_semaphore()

    def greet(device):
        pl.semaphore_signal(barrier, inc=1, device_id=device, device_id_type=MESH)

    for dz in (1, -1, 2, -2):
        greet(at_z(dz))
    for dx, dy in HALO:
        greet(at_xy(dx, dy))

    lane = lax.broadcasted_iota(jnp.int32, (8, 128), 1)
    depth = lax.rem(lane, 32)

    def joined(ref, x):
        return jnp.concatenate([ref[x, y].astype(F32) for y in range(4)], axis=1)

    loads[0].wait()
    for x in range(4):
        planes[x] = joined(x_ref, x)

    pl.semaphore_wait(barrier, 4 + len(HALO))

    def pass_token(n, device):
        pl.semaphore_signal(tokens.at[n], inc=1, device_id=device, device_id_type=MESH)

    def await_tokens(*ns):
        for n in ns:
            pl.semaphore_wait(tokens.at[n], 1)

    if quarter:
        pass_token(0, at_z(2))
        pass_token(1, at_z(-2))

    def copy(src, dst, send, recv, device):
        return pltpu.make_async_remote_copy(
            src_ref=src, dst_ref=dst, send_sem=send, recv_sem=recv, device_id=device, device_id_type=MESH
        )

    halo = []
    for h, (dx, dy) in enumerate(HALO):
        first, count = {-1: (0, 1), 0: (0, 4), 1: (3, 1)}[dx]
        halo.append(
            copy(
                planes.at[pl.ds(first, count)], rim.at[h, pl.ds(0, count)],
                halo_s.at[h], halo_r.at[h], at_xy(dx, dy),
            )
        )
        halo[-1].start()
    loads[1].wait()
    weight = jnp.concatenate([w_ref[...].astype(F32), jnp.zeros((8, chans), F32)], axis=0).astype(BF16)
    if quarter:
        await_tokens(0, 1)
        pass_token(2, at_z(4))
        pass_token(3, at_z(-4))
    for one in halo:
        one.wait_recv()
    if ny > 4:
        pass_token(4, at_xy(0, 2))
        pass_token(5, at_xy(0, -2))
    if quarter:
        await_tokens(2, 3)
        pass_token(6, at_z(8))
        pass_token(7, at_z(-8))

    inside_x = {-1: ix < nx - 1, 0: None, 1: ix > 0}
    inside_y = {-1: iy < ny - 1, 0: None, 1: iy > 0}

    def guarded(value, dx, dy):
        for ok in (inside_x[dx], inside_y[dy]):
            if ok is not None:
                value = jnp.where(ok, value, 0.0)
        return value

    def beside(plane, dy):
        if plane == 0 or plane == 5:
            dx = -1 if plane == 0 else 1
            return guarded(rim[HALO.index((-dx, -dy)), 0], -dx, -dy)
        if dy == 0:
            return planes[plane - 1]
        return guarded(rim[HALO.index((0, -dy)), plane - 1], 0, -dy)

    shifted = {}
    for plane in range(6):
        centre = beside(plane, 0)
        below = jnp.where(lane < 32, pltpu.roll(beside(plane, -1), 32, 1), pltpu.roll(centre, 32, 1))
        above = jnp.where(lane >= 96, pltpu.roll(beside(plane, 1), 96, 1), pltpu.roll(centre, 96, 1))
        for b, value in enumerate((below, centre, above)):
            shifted[plane, b, 0] = jnp.where(depth > 0, pltpu.roll(value, 1, 1), 0.0)
            shifted[plane, b, 1] = value
            shifted[plane, b, 2] = jnp.where(depth < 31, pltpu.roll(value, 127, 1), 0.0)
    rows = []
    for a in range(3):
        for b in range(3):
            for c in range(3):
                rows.append(jnp.concatenate([shifted[x + a, b, c] for x in range(4)], axis=1))
    ones = jnp.where(lax.broadcasted_iota(jnp.int32, (8, 512), 0) == 0, 1.0, 0.0)
    patches = jnp.concatenate(rows + [ones], axis=0).astype(BF16)

    partial = lax.dot_general(weight, patches, (((0,), (0,)), ((), ())), preferred_element_type=F32)

    def folded(block):
        width = block.shape[1] // 2
        return jnp.concatenate([block[:, :width], block[:, width:]], axis=0)

    turn = half + quarter
    for owner in range(nz):
        way = lax.rem(owner - iz + nz, CLASSES)
        apart = owner - iz - jnp.where(way == 0, CLASSES, way) + CLASSES * turn + nz
        block = partial[owner * 8 : owner * 8 + 8]
        part[way, lax.rem(lax.div(apart, CLASSES), groups)] = folded(block).astype(BF16)

    order = sorted(range(-half, half), key=lambda j: -abs(4 * j + 2))
    outer, inner = order[: 2 * quarter], order[2 * quarter :]
    batches = [outer, inner]
    sources = [(1, None), (-1, None), (2, range(0, half)), (-2, range(1 - half, 1))]

    def slot_of(j):
        return (j + turn) % groups

    def owner_group(device, j):
        return lax.div(lax.rem(iz + device + 4 * j + 2 + nz, nz), CLASSES)

    stage = {}
    for n, batch in enumerate(batches):
        for s, (dz, members) in enumerate(sources):
            slots = sorted(slot_of(j) for j in batch if members is None or j in members)
            if slots:
                assert slots == list(range(slots[0], slots[0] + len(slots)))
                stage[s, n] = copy(
                    part.at[(3, 1, 0, 0)[s], pl.ds(slots[0] - (s == 3), len(slots))],
                    near.at[s, pl.ds(slots[0], len(slots))],
                    rs1_s.at[s, n], rs1_r.at[s, n], at_z(dz),
                )
                stage[s, n].start()

    if quarter:
        await_tokens(6, 7)

    sent = list(halo)
    far_in = []
    for n, batch in enumerate(batches):
        for s in range(4):
            if (s, n) in stage:
                stage[s, n].wait_recv()
        for j in batch:
            value = part[2, slot_of(j)].astype(F32)
            for s, (dz, members) in enumerate(sources):
                if members is None or j in members:
                    value = value + near[s, slot_of(j)].astype(F32)
            acc[j + half] = value.astype(BF16)
            one = copy(acc.at[j + half], far.at[j + half], rs2_s.at[j + half], rs2_r.at[j + half], at_z(4 * j + 2))
            one.start()
            far_in.insert(0, (j, one))
            sent.append(one)

    square = lax.broadcasted_iota(jnp.int32, (8, 8), 0) == lax.broadcasted_iota(jnp.int32, (8, 8), 1)
    loads[3].wait()
    spread = jnp.broadcast_to(bias_ref[...].astype(F32), (8, 8))
    column = jnp.sum(jnp.where(square, spread, 0.0), axis=1, keepdims=True)
    pre = jnp.concatenate([column, column], axis=0)
    loads[2].wait()
    cot = folded(jnp.concatenate([joined(cot_ref, x) for x in range(4)], axis=1))
    for j, one in far_in:
        one.wait_recv()
        pre = pre + far[j + half].astype(F32)
    sig = jax.nn.sigmoid(pre)
    mine[...] = (cot * sig * (1.0 + pre * (1.0 - sig))).astype(BF16)

    for j in order:
        one = copy(mine, gath.at[cls, grp], ag1_s.at[j + half], ag1_r.at[j + half], at_z(4 * j + 2))
        one.start()
        sent.append(one)

    act = (pre * sig).astype(BF16)
    for x in range(4):
        for y in range(4):
            first = (x % 2) * 128 + y * 32
            act_ref[x, y] = act[(x // 2) * 8 : (x // 2) * 8 + 8, first : first + 32]
    stores = [pltpu.make_async_copy(act_ref, act_hbm, local.at[3])]
    stores[0].start()

    for j in reversed(order):
        slot = gath.at[held, owner_group(0, -j - 1)]
        copy(mine, slot, ag1_s.at[j + half], ag1_r.at[j + half], at_z(4 * j + 2)).wait_recv()
        for s, (dz, members) in enumerate(sources):
            if members is None or j in members:
                copy(slot, slot, ag2_s.at[s], ag2_r.at[s], at_z(dz)).start()
    for s, (dz, members) in enumerate(sources):
        span = gath.at[0] if members is None else gath.at[0, pl.ds(0, half)]
        copy(span, span, ag2_s.at[s], ag2_r.at[s], at_z(dz)).wait_recv()

    blocks = []
    for owner in range(nz):
        block = gath[owner % CLASSES, owner // CLASSES].astype(F32)
        blocks.append(jnp.concatenate([block[:8], block[8:]], axis=1))
    slope = jnp.concatenate(blocks, axis=0).astype(BF16)

    product = lax.dot_general(patches, slope, (((1,), (1,)), ((), ())), preferred_element_type=F32)
    size = 256 // peers
    for d in range(peers):
        top = min(max(224 - d * size, 0), size)
        lines = [product[d * size : d * size + top]] if top else []
        if top < size:
            lines.append(jnp.zeros((size - top, chans), F32))
        grad[d] = folded(jnp.concatenate(lines, axis=0)).astype(BF16)

    me = ix * ny + iy

    others = [(dx, dy) for dx in range(nx) for dy in range(ny) if (dx, dy) != (0, 0)]
    others.sort(key=lambda d: -(min(d[0], nx - d[0]) + (min(d[1], ny - d[1]) + 1) // 2))
    if ny > 4:
        await_tokens(4, 5)
    for n, (dx, dy) in enumerate(others):
        gx, gy, gz = at_xy(dx, dy)
        copy(grad.at[gx * ny + gy], pieces.at[n], wr_s, wr_r, (gx, gy, gz)).start()

    taps = jnp.dot(weight, slope, preferred_element_type=F32)

    def tap_rows(a, b, c, x):
        first = ((a * 3 + b) * 3 + c) * 8
        return taps[first : first + 8, x * 128 : x * 128 + 128]

    own = {}
    for plane in range(6):
        moved = []
        for b in range(3):
            by_depth = []
            for c in range(3):
                terms = [tap_rows(a, b, c, plane - a) for a in range(3) if 0 <= plane - a < 4]
                by_depth.append(functools.reduce(jnp.add, terms))
            moved.append(
                by_depth[1]
                + jnp.where(depth < 31, pltpu.roll(by_depth[0], 127, 1), 0.0)
                + jnp.where(depth > 0, pltpu.roll(by_depth[2], 1, 1), 0.0)
            )
        down, up = pltpu.roll(moved[0], 96, 1), pltpu.roll(moved[2], 32, 1)
        own[plane, 0] = moved[1] + jnp.where(lane < 96, down, 0.0) + jnp.where(lane >= 32, up, 0.0)
        own[plane, -1] = jnp.where(lane >= 96, down, 0.0)
        own[plane, 1] = jnp.where(lane < 32, up, 0.0)

    moves = []
    for h, (dx, dy) in enumerate(HALO):
        if dx == 0:
            for x in range(4):
                back[h, x] = own[x + 1, dy]
        else:
            back[h, 0] = own[0 if dx < 0 else 5, dy]
        count = 4 if dx == 0 else 1
        moves.append(
            copy(
                back.at[h, pl.ds(0, count)], back_in.at[h, pl.ds(0, count)],
                bk_s.at[h], bk_r.at[h], at_xy(dx, dy),
            )
        )
        moves[-1].start()

    copy(pieces, pieces, wr_s, wr_r, at_xy(0, 1)).wait_recv()
    whole = grad[me].astype(F32)
    for k in range(peers - 1):
        whole = whole + pieces[k].astype(F32)
    chunk[...] = (whole * factor).astype(BF16)
    for dx, dy in others:
        copy(chunk, total.at[me], wa_s, wa_r, at_xy(dx, dy)).start()
    stores.append(pltpu.make_async_copy(chunk, total.at[me], local.at[5]))
    stores[-1].start()

    for one in moves:
        one.wait_recv()
    sums = [own[x + 1, 0] for x in range(4)]
    for h, (dx, dy) in enumerate(HALO):
        if dx == 0:
            for x in range(4):
                sums[x] = sums[x] + guarded(back_in[h, x], dx, dy)
        else:
            x = 3 if dx < 0 else 0
            sums[x] = sums[x] + guarded(back_in[h, 0], dx, dy)
    for x in range(4):
        plane = sums[x].astype(BF16)
        for y in range(4):
            ig_ref[x, y] = plane[:, y * 32 : y * 32 + 32]
    stores.append(pltpu.make_async_copy(ig_ref, ig_hbm, local.at[4]))
    stores[-1].start()

    for one in sent + moves:
        one.wait_send()
    for one in stage.values():
        one.wait_send()
    for s, (dz, members) in enumerate(sources):
        span = gath.at[0] if members is None else gath.at[0, pl.ds(0, half)]
        copy(span, span, ag2_s.at[s], ag2_r.at[s], at_z(dz)).wait_send()

    rest = total.at[pl.ds(0, peers - 1)]
    copy(pieces, pieces, wr_s, wr_r, at_xy(0, 1)).wait_send()
    copy(rest, rest, wa_s, wa_r, at_xy(0, 1)).wait()
    for one in stores:
        one.wait()


def hand_on(size, act_in, ig_in, total, act, ig, wg, bg):
    chans = wg.shape[1]
    act[...] = act_in[...]
    ig[...] = ig_in[...]

    def chunk(d):
        value = total[d].astype(F32)
        return jnp.concatenate([value[:size], value[size:]], axis=1)

    for d in range(total.shape[0]):
        top = min(max(216 - d * size, 0), size)
        if top:
            wg[d * size : d * size + top] = chunk(d)[:top]
    line = jnp.broadcast_to(chunk(216 // size)[216 % size : 216 % size + 1], (8, chans))
    lane = lax.broadcasted_iota(jnp.int32, (8, chans), 1) - lax.axis_index("ch") * 8
    column = jnp.where(lane == lax.broadcasted_iota(jnp.int32, (8, chans), 0), line, 0.0)
    column = jnp.broadcast_to(jnp.sum(column, axis=1, keepdims=True), (8, 8))
    square = lax.broadcasted_iota(jnp.int32, (8, 8), 0) == lax.broadcasted_iota(jnp.int32, (8, 8), 1)
    bg[...] = jnp.sum(jnp.where(square, column, 0.0), axis=0, keepdims=True)


def body(nx, ny, nz, inputs, weight, bias, cotangent):
    groups = nz // CLASSES
    half = groups // 2
    peers = nx * ny
    chans = 8 * nz
    size = 256 // peers
    factor = 1.0 / math.sqrt(512 * peers)
    vmem = pl.BlockSpec(memory_space=pltpu.VMEM)
    hbm = pl.BlockSpec(memory_space=pl.ANY)
    sems = [(8,)] * 2 + [(4, 2)] * 2 + [(groups,)] * 4 + [(4,)] * 2 + [()] * 4 + [(8,)] * 2
    cells = jax.ShapeDtypeStruct((4, 4, 8, 32), BF16)
    gathered = jax.ShapeDtypeStruct((peers, 2 * size, chans // 2), BF16)
    results = pl.pallas_call(
        functools.partial(kernel, nx, ny, nz, factor),
        out_shape=(cells, cells, gathered),
        in_specs=[hbm] * 4,
        out_specs=(hbm,) * 3,
        scratch_shapes=[
            pltpu.VMEM((4, 4, 8, 32), BF16),
            pltpu.VMEM((216, chans), BF16),
            pltpu.VMEM((1, 8), BF16),
            pltpu.VMEM((4, 4, 8, 32), BF16),
            pltpu.VMEM((4, 4, 8, 32), BF16),
            pltpu.VMEM((4, 4, 8, 32), BF16),
            pltpu.VMEM((4, 8, 128), F32),
            pltpu.VMEM((8, 4, 8, 128), F32),
            pltpu.VMEM((CLASSES, groups, 16, 256), BF16),
            pltpu.VMEM((4, groups, 16, 256), BF16),
            pltpu.VMEM((groups, 16, 256), BF16),
            pltpu.VMEM((groups, 16, 256), BF16),
            pltpu.VMEM((16, 256), BF16),
            pltpu.VMEM((CLASSES, groups, 16, 256), BF16),
            pltpu.VMEM((peers, 2 * size, chans // 2), BF16),
            pltpu.VMEM((peers - 1, 2 * size, chans // 2), BF16),
            pltpu.VMEM((2 * size, chans // 2), BF16),
            pltpu.VMEM((8, 4, 8, 128), F32),
            pltpu.VMEM((8, 4, 8, 128), F32),
            pltpu.SemaphoreType.DMA((6,)),
            pltpu.SemaphoreType.REGULAR((8,)),
        ]
        + [pltpu.SemaphoreType.DMA(n) for n in sems],
        compiler_params=pltpu.CompilerParams(collective_id=0, has_side_effects=True),
    )(
        jnp.transpose(inputs, (0, 1, 3, 2)),
        weight.reshape(216, chans),
        bias.reshape(1, 8),
        jnp.transpose(cotangent, (0, 1, 3, 2)),
    )
    act, grad_in, grad_w, grad_b = pl.pallas_call(
        functools.partial(hand_on, size),
        out_shape=(cells, cells, jax.ShapeDtypeStruct((216, chans), F32), jax.ShapeDtypeStruct((1, 8), F32)),
        in_specs=[vmem] * 3,
        out_specs=(vmem,) * 4,
    )(*results)
    return (
        jnp.transpose(act, (0, 1, 3, 2)),
        jnp.transpose(grad_in, (0, 1, 3, 2)),
        grad_w.reshape(3, 3, 3, 8, chans),
        grad_b.reshape(8),
    )


def solution(mesh):
    sizes = (mesh.shape["gx"], mesh.shape["gy"], mesh.shape["ch"])
    return jax.shard_map(
        functools.partial(body, *sizes),
        mesh=mesh,
        in_specs=(
            P("gx", "gy", None, "ch"),
            P(None, None, None, "ch", None),
            P("ch"),
            P("gx", "gy", None, "ch"),
        ),
        out_specs=(
            P("gx", "gy", None, "ch"),
            P("gx", "gy", None, "ch"),
            P(None, None, None, "ch", None),
            P("ch"),
        ),
        check_vma=False,
    )
```

```python
import functools
import math

import jax
import jax.numpy as jnp
from jax import lax
from jax.experimental import pallas as pl
from jax.experimental.pallas import tpu as pltpu
from jax.sharding import PartitionSpec as P

MESH = pl.DeviceIdType.MESH
CLASSES = 4
HALO = [(dx, dy) for dx in (-1, 0, 1) for dy in (-1, 0, 1) if (dx, dy) != (0, 0)]
F32 = jnp.float32
BF16 = jnp.bfloat16


def kernel(
    nx, ny, nz, factor,
    x_hbm, w_hbm, bias_hbm, cot_hbm,
    act_hbm, ig_hbm, total,
    x_ref, w_ref, bias_ref, cot_ref, act_ref, ig_ref,
    planes, rim, part, near, acc, far, mine, gath, grad, pieces, chunk, back, back_in,
    local, tokens, halo_s, halo_r, rs1_s, rs1_r, rs2_s, rs2_r, ag1_s, ag1_r, ag2_s, ag2_r,
    wr_s, wr_r, wa_s, wa_r, bk_s, bk_r,
):
    ix, iy, iz = lax.axis_index("gx"), lax.axis_index("gy"), lax.axis_index("ch")
    groups = nz // CLASSES
    half = groups // 2
    quarter = half // 2
    peers = nx * ny
    chans = 8 * nz
    cls, grp = lax.rem(iz, CLASSES), lax.div(iz, CLASSES)
    held = lax.rem(cls + 2, CLASSES)

    loads = [
        pltpu.make_async_copy(src, dst, local.at[n])
        for n, (src, dst) in enumerate(((x_hbm, x_ref), (w_hbm, w_ref), (cot_hbm, cot_ref), (bias_hbm, bias_ref)))
    ]
    for one in loads:
        one.start()

    def at_xy(dx, dy):
        return (lax.rem(ix + dx + nx, nx), lax.rem(iy + dy + ny, ny), iz)

    def at_z(dz):
        return (ix, iy, lax.rem(iz + dz + nz, nz))

    barrier = pltpu.get_barrier_semaphore()

    def greet(device):
        pl.semaphore_signal(barrier, inc=1, device_id=device, device_id_type=MESH)

    for dz in (1, -1, 2, -2):
        greet(at_z(dz))
    for dx, dy in HALO:
        greet(at_xy(dx, dy))

    lane = lax.broadcasted_iota(jnp.int32, (8, 128), 1)
    depth = lax.rem(lane, 32)

    def joined(ref, x):
        return jnp.concatenate([ref[x, y].astype(F32) for y in range(4)], axis=1)

    loads[0].wait()
    for x in range(4):
        planes[x] = joined(x_ref, x).astype(BF16)

    pl.semaphore_wait(barrier, 4 + len(HALO))

    def pass_token(n, device):
        pl.semaphore_signal(tokens.at[n], inc=1, device_id=device, device_id_type=MESH)

    def await_tokens(*ns):
        for n in ns:
            pl.semaphore_wait(tokens.at[n], 1)

    if quarter:
        pass_token(0, at_z(2))
        pass_token(1, at_z(-2))

    def copy(src, dst, send, recv, device):
        return pltpu.make_async_remote_copy(
            src_ref=src, dst_ref=dst, send_sem=send, recv_sem=recv, device_id=device, device_id_type=MESH
        )

    halo = []
    for h, (dx, dy) in enumerate(HALO):
        first, count = {-1: (0, 1), 0: (0, 4), 1: (3, 1)}[dx]
        halo.append(
            copy(
                planes.at[pl.ds(first, count)], rim.at[h, pl.ds(0, count)],
                halo_s.at[h], halo_r.at[h], at_xy(dx, dy),
            )
        )
        halo[-1].start()
    loads[1].wait()
    weight = jnp.concatenate([w_ref[...].astype(F32), jnp.zeros((8, chans), F32)], axis=0).astype(BF16)
    if quarter:
        await_tokens(0, 1)
        pass_token(2, at_z(4))
        pass_token(3, at_z(-4))
    for one in halo:
        one.wait_recv()
    if ny > 4:
        pass_token(4, at_xy(0, 2))
        pass_token(5, at_xy(0, -2))
    if quarter:
        await_tokens(2, 3)
        pass_token(6, at_z(8))
        pass_token(7, at_z(-8))

    inside_x = {-1: ix < nx - 1, 0: None, 1: ix > 0}
    inside_y = {-1: iy < ny - 1, 0: None, 1: iy > 0}

    def guarded(value, dx, dy):
        for ok in (inside_x[dx], inside_y[dy]):
            if ok is not None:
                value = jnp.where(ok, value, 0.0)
        return value

    def beside(plane, dy):
        if plane == 0 or plane == 5:
            dx = -1 if plane == 0 else 1
            return guarded(rim[HALO.index((-dx, -dy)), 0].astype(F32), -dx, -dy)
        if dy == 0:
            return planes[plane - 1].astype(F32)
        return guarded(rim[HALO.index((0, -dy)), plane - 1].astype(F32), 0, -dy)

    shifted = {}
    for plane in range(6):
        centre = beside(plane, 0)
        below = jnp.where(lane < 32, pltpu.roll(beside(plane, -1), 32, 1), pltpu.roll(centre, 32, 1))
        above = jnp.where(lane >= 96, pltpu.roll(beside(plane, 1), 96, 1), pltpu.roll(centre, 96, 1))
        for b, value in enumerate((below, centre, above)):
            shifted[plane, b, 0] = jnp.where(depth > 0, pltpu.roll(value, 1, 1), 0.0)
            shifted[plane, b, 1] = value
            shifted[plane, b, 2] = jnp.where(depth < 31, pltpu.roll(value, 127, 1), 0.0)
    rows = []
    for a in range(3):
        for b in range(3):
            for c in range(3):
                rows.append(jnp.concatenate([shifted[x + a, b, c] for x in range(4)], axis=1))
    ones = jnp.where(lax.broadcasted_iota(jnp.int32, (8, 512), 0) == 0, 1.0, 0.0)
    patches = jnp.concatenate(rows + [ones], axis=0).astype(BF16)

    partial = lax.dot_general(weight, patches, (((0,), (0,)), ((), ())), preferred_element_type=F32)

    def folded(block):
        width = block.shape[1] // 2
        return jnp.concatenate([block[:, :width], block[:, width:]], axis=0)

    turn = half + quarter
    for owner in range(nz):
        way = lax.rem(owner - iz + nz, CLASSES)
        apart = owner - iz - jnp.where(way == 0, CLASSES, way) + CLASSES * turn + nz
        block = partial[owner * 8 : owner * 8 + 8]
        part[way, lax.rem(lax.div(apart, CLASSES), groups)] = folded(block).astype(BF16)

    order = sorted(range(-half, half), key=lambda j: -abs(4 * j + 2))
    outer, inner = order[: 2 * quarter], order[2 * quarter :]
    batches = [outer, inner]
    sources = [(1, None), (-1, None), (2, range(0, half)), (-2, range(1 - half, 1))]

    def slot_of(j):
        return (j + turn) % groups

    def owner_group(device, j):
        return lax.div(lax.rem(iz + device + 4 * j + 2 + nz, nz), CLASSES)

    stage = {}
    for n, batch in enumerate(batches):
        for s, (dz, members) in enumerate(sources):
            slots = sorted(slot_of(j) for j in batch if members is None or j in members)
            if slots:
                assert slots == list(range(slots[0], slots[0] + len(slots)))
                stage[s, n] = copy(
                    part.at[(3, 1, 0, 0)[s], pl.ds(slots[0] - (s == 3), len(slots))],
                    near.at[s, pl.ds(slots[0], len(slots))],
                    rs1_s.at[s, n], rs1_r.at[s, n], at_z(dz),
                )
                stage[s, n].start()

    if quarter:
        await_tokens(6, 7)

    sent = list(halo)
    far_in = []
    for n, batch in enumerate(batches):
        for s in range(4):
            if (s, n) in stage:
                stage[s, n].wait_recv()
        for j in batch:
            value = part[2, slot_of(j)].astype(F32)
            for s, (dz, members) in enumerate(sources):
                if members is None or j in members:
                    value = value + near[s, slot_of(j)].astype(F32)
            acc[j + half] = value.astype(BF16)
            one = copy(acc.at[j + half], far.at[j + half], rs2_s.at[j + half], rs2_r.at[j + half], at_z(4 * j + 2))
            one.start()
            far_in.insert(0, (j, one))
            sent.append(one)

    square = lax.broadcasted_iota(jnp.int32, (8, 8), 0) == lax.broadcasted_iota(jnp.int32, (8, 8), 1)
    loads[3].wait()
    spread = jnp.broadcast_to(bias_ref[...].astype(F32), (8, 8))
    column = jnp.sum(jnp.where(square, spread, 0.0), axis=1, keepdims=True)
    pre = jnp.concatenate([column, column], axis=0)
    loads[2].wait()
    cot = folded(jnp.concatenate([joined(cot_ref, x) for x in range(4)], axis=1))
    for j, one in far_in:
        one.wait_recv()
        pre = pre + far[j + half].astype(F32)
    sig = jax.nn.sigmoid(pre)
    mine[...] = (cot * sig * (1.0 + pre * (1.0 - sig))).astype(BF16)

    for j in order:
        one = copy(mine, gath.at[cls, grp], ag1_s.at[j + half], ag1_r.at[j + half], at_z(4 * j + 2))
        one.start()
        sent.append(one)

    act = (pre * sig).astype(BF16)
    for x in range(4):
        for y in range(4):
            first = (x % 2) * 128 + y * 32
            act_ref[x, y] = act[(x // 2) * 8 : (x // 2) * 8 + 8, first : first + 32]
    stores = [pltpu.make_async_copy(act_ref, act_hbm, local.at[3])]
    stores[0].start()

    for j in reversed(order):
        slot = gath.at[held, owner_group(0, -j - 1)]
        copy(mine, slot, ag1_s.at[j + half], ag1_r.at[j + half], at_z(4 * j + 2)).wait_recv()
        for s, (dz, members) in enumerate(sources):
            if members is None or j in members:
                copy(slot, slot, ag2_s.at[s], ag2_r.at[s], at_z(dz)).start()
    for s, (dz, members) in enumerate(sources):
        span = gath.at[0] if members is None else gath.at[0, pl.ds(0, half)]
        copy(span, span, ag2_s.at[s], ag2_r.at[s], at_z(dz)).wait_recv()

    blocks = []
    for owner in range(nz):
        block = gath[owner % CLASSES, owner // CLASSES].astype(F32)
        blocks.append(jnp.concatenate([block[:8], block[8:]], axis=1))
    slope = jnp.concatenate(blocks, axis=0).astype(BF16)

    product = lax.dot_general(patches, slope, (((1,), (1,)), ((), ())), preferred_element_type=F32)
    size = 256 // peers
    for d in range(peers):
        top = min(max(224 - d * size, 0), size)
        lines = [product[d * size : d * size + top]] if top else []
        if top < size:
            lines.append(jnp.zeros((size - top, chans), F32))
        grad[d] = folded(jnp.concatenate(lines, axis=0)).astype(BF16)

    me = ix * ny + iy

    others = [(dx, dy) for dx in range(nx) for dy in range(ny) if (dx, dy) != (0, 0)]
    others.sort(key=lambda d: -(min(d[0], nx - d[0]) + (min(d[1], ny - d[1]) + 1) // 2))
    if ny > 4:
        await_tokens(4, 5)
    for n, (dx, dy) in enumerate(others):
        gx, gy, gz = at_xy(dx, dy)
        copy(grad.at[gx * ny + gy], pieces.at[n], wr_s, wr_r, (gx, gy, gz)).start()

    taps = jnp.dot(weight, slope, preferred_element_type=F32)

    def tap_rows(a, b, c, x):
        first = ((a * 3 + b) * 3 + c) * 8
        return taps[first : first + 8, x * 128 : x * 128 + 128]

    own = {}
    for plane in range(6):
        moved = []
        for b in range(3):
            by_depth = []
            for c in range(3):
                terms = [tap_rows(a, b, c, plane - a) for a in range(3) if 0 <= plane - a < 4]
                by_depth.append(functools.reduce(jnp.add, terms))
            moved.append(
                by_depth[1]
                + jnp.where(depth < 31, pltpu.roll(by_depth[0], 127, 1), 0.0)
                + jnp.where(depth > 0, pltpu.roll(by_depth[2], 1, 1), 0.0)
            )
        down, up = pltpu.roll(moved[0], 96, 1), pltpu.roll(moved[2], 32, 1)
        own[plane, 0] = moved[1] + jnp.where(lane < 96, down, 0.0) + jnp.where(lane >= 32, up, 0.0)
        own[plane, -1] = jnp.where(lane >= 96, down, 0.0)
        own[plane, 1] = jnp.where(lane < 32, up, 0.0)

    moves = []
    for h, (dx, dy) in enumerate(HALO):
        if dx == 0:
            for x in range(4):
                back[h, x] = own[x + 1, dy]
        else:
            back[h, 0] = own[0 if dx < 0 else 5, dy]
        count = 4 if dx == 0 else 1
        moves.append(
            copy(
                back.at[h, pl.ds(0, count)], back_in.at[h, pl.ds(0, count)],
                bk_s.at[h], bk_r.at[h], at_xy(dx, dy),
            )
        )
        moves[-1].start()

    copy(pieces, pieces, wr_s, wr_r, at_xy(0, 1)).wait_recv()
    whole = grad[me].astype(F32)
    for k in range(peers - 1):
        whole = whole + pieces[k].astype(F32)
    chunk[...] = (whole * factor).astype(BF16)
    for dx, dy in others:
        copy(chunk, total.at[me], wa_s, wa_r, at_xy(dx, dy)).start()
    stores.append(pltpu.make_async_copy(chunk, total.at[me], local.at[5]))
    stores[-1].start()

    for one in moves:
        one.wait_recv()
    sums = [own[x + 1, 0] for x in range(4)]
    for h, (dx, dy) in enumerate(HALO):
        if dx == 0:
            for x in range(4):
                sums[x] = sums[x] + guarded(back_in[h, x], dx, dy)
        else:
            x = 3 if dx < 0 else 0
            sums[x] = sums[x] + guarded(back_in[h, 0], dx, dy)
    for x in range(4):
        plane = sums[x].astype(BF16)
        for y in range(4):
            ig_ref[x, y] = plane[:, y * 32 : y * 32 + 32]
    stores.append(pltpu.make_async_copy(ig_ref, ig_hbm, local.at[4]))
    stores[-1].start()

    for one in sent + moves:
        one.wait_send()
    for one in stage.values():
        one.wait_send()
    for s, (dz, members) in enumerate(sources):
        span = gath.at[0] if members is None else gath.at[0, pl.ds(0, half)]
        copy(span, span, ag2_s.at[s], ag2_r.at[s], at_z(dz)).wait_send()

    rest = total.at[pl.ds(0, peers - 1)]
    copy(pieces, pieces, wr_s, wr_r, at_xy(0, 1)).wait_send()
    copy(rest, rest, wa_s, wa_r, at_xy(0, 1)).wait()
    for one in stores:
        one.wait()


def hand_on(size, act_in, ig_in, total, act, ig, wg, bg):
    chans = wg.shape[1]
    act[...] = act_in[...]
    ig[...] = ig_in[...]

    def chunk(d):
        value = total[d].astype(F32)
        return jnp.concatenate([value[:size], value[size:]], axis=1)

    for d in range(total.shape[0]):
        top = min(max(216 - d * size, 0), size)
        if top:
            wg[d * size : d * size + top] = chunk(d)[:top]
    line = jnp.broadcast_to(chunk(216 // size)[216 % size : 216 % size + 1], (8, chans))
    lane = lax.broadcasted_iota(jnp.int32, (8, chans), 1) - lax.axis_index("ch") * 8
    column = jnp.where(lane == lax.broadcasted_iota(jnp.int32, (8, chans), 0), line, 0.0)
    column = jnp.broadcast_to(jnp.sum(column, axis=1, keepdims=True), (8, 8))
    square = lax.broadcasted_iota(jnp.int32, (8, 8), 0) == lax.broadcasted_iota(jnp.int32, (8, 8), 1)
    bg[...] = jnp.sum(jnp.where(square, column, 0.0), axis=0, keepdims=True)


def body(nx, ny, nz, inputs, weight, bias, cotangent):
    groups = nz // CLASSES
    half = groups // 2
    peers = nx * ny
    chans = 8 * nz
    size = 256 // peers
    factor = 1.0 / math.sqrt(512 * peers)
    vmem = pl.BlockSpec(memory_space=pltpu.VMEM)
    anywhere = pl.BlockSpec(memory_space=pl.ANY)
    sems = [(8,)] * 2 + [(4, 2)] * 2 + [(groups,)] * 4 + [(4,)] * 2 + [()] * 4 + [(8,)] * 2
    cells = jax.ShapeDtypeStruct((4, 4, 8, 32), BF16)
    gathered = jax.ShapeDtypeStruct((peers, 2 * size, chans // 2), BF16)
    results = pl.pallas_call(
        functools.partial(kernel, nx, ny, nz, factor),
        out_shape=(cells, cells, gathered),
        in_specs=[pl.BlockSpec(memory_space=pltpu.HBM)] * 4,
        out_specs=(anywhere,) * 3,
        scratch_shapes=[
            pltpu.VMEM((4, 4, 8, 32), BF16),
            pltpu.VMEM((216, chans), BF16),
            pltpu.VMEM((1, 8), BF16),
            pltpu.VMEM((4, 4, 8, 32), BF16),
            pltpu.VMEM((4, 4, 8, 32), BF16),
            pltpu.VMEM((4, 4, 8, 32), BF16),
            pltpu.VMEM((4, 8, 128), BF16),
            pltpu.VMEM((8, 4, 8, 128), BF16),
            pltpu.VMEM((CLASSES, groups, 16, 256), BF16),
            pltpu.VMEM((4, groups, 16, 256), BF16),
            pltpu.VMEM((groups, 16, 256), BF16),
            pltpu.VMEM((groups, 16, 256), BF16),
            pltpu.VMEM((16, 256), BF16),
            pltpu.VMEM((CLASSES, groups, 16, 256), BF16),
            pltpu.VMEM((peers, 2 * size, chans // 2), BF16),
            pltpu.VMEM((peers - 1, 2 * size, chans // 2), BF16),
            pltpu.VMEM((2 * size, chans // 2), BF16),
            pltpu.VMEM((8, 4, 8, 128), F32),
            pltpu.VMEM((8, 4, 8, 128), F32),
            pltpu.SemaphoreType.DMA((6,)),
            pltpu.SemaphoreType.REGULAR((8,)),
        ]
        + [pltpu.SemaphoreType.DMA(n) for n in sems],
        compiler_params=pltpu.CompilerParams(collective_id=0, has_side_effects=True, vmem_limit_bytes=16 << 20),
    )(
        *(
            pltpu.with_memory_space_constraint(array, pltpu.HBM)
            for array in (
                jnp.transpose(inputs, (0, 1, 3, 2)),
                weight.reshape(216, chans),
                bias.reshape(1, 8),
                jnp.transpose(cotangent, (0, 1, 3, 2)),
            )
        )
    )
    act, grad_in, grad_w, grad_b = pl.pallas_call(
        functools.partial(hand_on, size),
        out_shape=(cells, cells, jax.ShapeDtypeStruct((216, chans), F32), jax.ShapeDtypeStruct((1, 8), F32)),
        in_specs=[vmem] * 3,
        compiler_params=pltpu.CompilerParams(vmem_limit_bytes=8 << 20),
        out_specs=(vmem,) * 4,
    )(*results)
    return (
        jnp.transpose(act, (0, 1, 3, 2)),
        jnp.transpose(grad_in, (0, 1, 3, 2)),
        grad_w.reshape(3, 3, 3, 8, chans),
        grad_b.reshape(8),
    )


def solution(mesh):
    sizes = (mesh.shape["gx"], mesh.shape["gy"], mesh.shape["ch"])
    return jax.shard_map(
        functools.partial(body, *sizes),
        mesh=mesh,
        in_specs=(
            P("gx", "gy", None, "ch"),
            P(None, None, None, "ch", None),
            P("ch"),
            P("gx", "gy", None, "ch"),
        ),
        out_specs=(
            P("gx", "gy", None, "ch"),
            P("gx", "gy", None, "ch"),
            P(None, None, None, "ch", None),
            P("ch"),
        ),
        check_vma=False,
    )
```
